128 devices in a mesh: pipe: 8 (over y_lo, x), ctx: 16 (over y_hi, z, core).
Axes of the slice: x: 4, y: 4 (y_hi: 2, y_lo: 2; y = y_hi * 2 + y_lo), z: 4, core: 2. Of those that a mesh axis runs over, the one named last changes fastest.
Arguments:
- queries: bfloat16 [8, 8192, 1024], P('pipe', 'ctx'), may hold values from -14 to 14
- keys: bfloat16 [8, 8192, 128], P('pipe', 'ctx'), may hold values from -14 to 14
- values: bfloat16 [8, 8192, 128], P('pipe', 'ctx'), may hold values from -6 to 6
- out_grad: bfloat16 [8, 8192, 1024], P('pipe', 'ctx'), may hold values from -6 to 6
- doc_lengths: int32 [8, 8], P('pipe'), may hold values from 1 to 4096, 8192 in all within a row
- assignment: int32 [8, 16], P('pipe'), may hold values from 0 to 15, each once within a row
Outputs:
- q_grad_in: bfloat16 [8, 8192, 1024], P('pipe', 'ctx')
- k_grad_in: bfloat16 [8, 8192, 128], P('pipe', 'ctx')
- v_grad_in: bfloat16 [8, 8192, 128], P('pipe', 'ctx')
The draws below stay inside these ranges and needn't reach their ends.
Inputs may be any that keep to these rules, and one draw needn't show every extreme that they name: Each row is a permutation; device i of ctx holds the blocks assignment[s, i] and 31 - assignment[s, i] of 256 positions, in that order. `doc_lengths`: each row sums to 8192 and its largest entry is 4096.
All inputs are finite; a program needn't handle non-finite values.
Results may differ from the reference program's by a relative error of at most 0.0069.
Values may be sent and summed in bfloat16 or wider, within the bound.
No kernel may reach another device: no remote copies, remote signals or barrier semaphores. Data moves between devices by JAX's collectives and lax.ppermute only.
A program may use at most 128 MiB of HBM per device.

```python
import math
import jax
import jax.numpy as jnp
import numpy as np
from jax import lax

BLOCK = 256
HQ = 8
HD = 128
DOCS = 8
LENGTH = 8192
MOST = 4096
SECTIONS = 8
N_CTX = 16


def draw_queries(key, part):
    drawn = jnp.clip(jax.random.normal(jax.random.fold_in(key, 21), (SECTIONS, LENGTH, HQ * HD), jnp.float32), -5.0, 5.0)
    return drawn.astype(jnp.bfloat16)


def draw_keys(key, part):
    drawn = jnp.clip(jax.random.normal(jax.random.fold_in(key, 31), (SECTIONS, LENGTH, HD), jnp.float32), -5.0, 5.0)
    return drawn.astype(jnp.bfloat16)


def level_of(own_key, dims, cuts, low, largest):
    def one(dim, parts):
        steps = jax.random.uniform(jax.random.fold_in(jax.random.fold_in(own_key, 6), dim), (parts,), jnp.float32, low / len(cuts), largest / len(cuts))
        return jnp.repeat(jnp.exp(steps), dims[dim] // parts).reshape((-1,) + (1,) * (len(dims) - dim - 1))

    factor_of = one(*cuts[0])
    for cut in cuts[1:]:
        factor_of = factor_of * one(*cut)
    return factor_of


def profile(count, total, bound, skew):
    loads = [(1 << 20) // math.isqrt(rank ** skew) + 1 for rank in range(2, count + 1)]
    surplus, given = total - bound - (count - 1), [1] * (count - 1)
    while surplus > 0:
        free = [i for i in range(count - 1) if given[i] < bound]
        pool, remaining = sum([loads[i] for i in free]), surplus
        for i in free:
            more = min(bound - given[i], max(1, remaining * loads[i] // pool), surplus)
            given[i] = given[i] + more
            surplus = surplus - more
    return np.array([bound] + given)


def ragged_sizes(own_key, amount, total, limit, skew):
    if amount == 2:
        one = jax.random.randint(own_key, (), max(1, total - limit), min(limit, total - 1) + 1)
        return jnp.stack([one, total - one])
    tallies = jnp.asarray(profile(amount, total, limit, skew), jnp.int32)
    twos = (amount - 1) // 2
    donor, receiver = tallies[1:1 + 2 * twos:2], tallies[2:2 + 2 * twos:2]
    room = jnp.minimum(donor - 1, limit - receiver)
    passed = jax.random.randint(jax.random.fold_in(own_key, 1), (twos,), 0, 1 << 20) % (room + 1)
    tallies = tallies.at[1:1 + 2 * twos:2].set(donor - passed).at[2:2 + 2 * twos:2].set(receiver + passed)
    return tallies[jax.random.permutation(jax.random.fold_in(own_key, 2), amount)]


def centred(own_key, shape, scale, reach, split=(), kind=jnp.bfloat16):
    drawn = scale * jax.random.normal(own_key, shape, jnp.float32)
    if split:
        drawn = drawn * level_of(own_key, shape, split, -0.22, 0.18)
    return jnp.clip(drawn, -reach, reach).astype(kind)


def setup_inputs(seed: int = 0) -> dict:
    arg_keys = jax.random.split(jax.random.key(seed), 7)
    queries = draw_queries(jax.random.fold_in(arg_keys[6], 71), 0)
    keys = draw_keys(jax.random.fold_in(arg_keys[6], 71), 0)
    values = centred(arg_keys[2], (SECTIONS, LENGTH, HD), 1.0, 6.0, ((0, 8), (1, 16)))
    out_grad = centred(arg_keys[3], (SECTIONS, LENGTH, HQ * HD), 1.0, 6.0, ((0, 8), (1, 16)))
    doc_lengths = jax.vmap(lambda own: ragged_sizes(own, DOCS, LENGTH, MOST, 2))(jax.random.split(arg_keys[4], SECTIONS)).reshape((SECTIONS, DOCS)).astype(jnp.int32)
    assignment = jax.vmap(lambda own: jax.random.permutation(own, N_CTX))(jax.random.split(arg_keys[5], SECTIONS)).reshape((SECTIONS, N_CTX)).astype(jnp.int32)
    return dict(queries=queries, keys=keys, values=values, out_grad=out_grad, doc_lengths=doc_lengths, assignment=assignment)


def doc_index(position, doc_starts):
    return lax.optimization_barrier(jnp.sum((position[..., None] >= doc_starts).astype(jnp.int32), axis=-1)) - 1

def section_backward(queries, keys, values, out_grad, doc_sizes, placing):
    stored_rows = jnp.arange(LENGTH, dtype=jnp.int32)
    device_of = stored_rows // (2 * BLOCK)
    half_of = stored_rows // BLOCK % 2
    own_block = placing[device_of].astype(jnp.int32)
    block_id = jnp.where(half_of == 0, own_block, 2 * N_CTX - 1 - own_block)
    position = (block_id * BLOCK + stored_rows % BLOCK).astype(jnp.int32)
    sorted_from = jnp.zeros((LENGTH,), jnp.int32).at[position].set(stored_rows)
    query_sorted = queries[sorted_from]
    key_sorted = keys[sorted_from]
    value_sorted = values[sorted_from]
    grad_sorted = out_grad[sorted_from]
    doc_starts = (jnp.cumsum(doc_sizes) - doc_sizes).astype(jnp.int32)
    doc_all = doc_index(jnp.arange(LENGTH, dtype=jnp.int32), doc_starts)
    score_scale = 1.0 / math.sqrt(HD)
    window = MOST + BLOCK

    def one_block(loop_state, block_number):
        key_acc, value_acc = loop_state
        first = (block_number * BLOCK).astype(jnp.int32)
        lowest = jnp.maximum(first - MOST, 0).astype(jnp.int32)
        query_tile = lax.dynamic_slice_in_dim(query_sorted, first, BLOCK, 0).reshape(BLOCK, HQ, HD).astype(jnp.float32)
        grad_tile = lax.dynamic_slice_in_dim(grad_sorted, first, BLOCK, 0).reshape(BLOCK, HQ, HD).astype(jnp.float32)
        key_window = lax.dynamic_slice_in_dim(key_sorted, lowest, window, 0).astype(jnp.float32)
        value_window = lax.dynamic_slice_in_dim(value_sorted, lowest, window, 0).astype(jnp.float32)
        query_pos = first + jnp.arange(BLOCK, dtype=jnp.int32)
        key_pos = lowest + jnp.arange(window, dtype=jnp.int32)
        query_doc = lax.dynamic_slice_in_dim(doc_all, first, BLOCK, 0)
        key_doc = lax.dynamic_slice_in_dim(doc_all, lowest, window, 0)
        allowed = (key_pos[None, :] <= query_pos[:, None]) & (key_doc[None, :] == query_doc[:, None])
        scores = jnp.einsum('qhd,kd->hqk', query_tile, key_window) * score_scale
        logsum = jax.nn.logsumexp(jnp.where(allowed[None], scores, -jnp.inf), axis=-1)
        softmax = jnp.where(allowed[None], jnp.exp(scores - logsum[..., None]), 0.0)
        grad_probs = jnp.einsum('qhd,kd->hqk', grad_tile, value_window)
        row_delta = lax.optimization_barrier(jnp.sum(softmax * grad_probs, axis=-1))
        grad_scores = lax.optimization_barrier((softmax * (grad_probs - row_delta[..., None])).astype(jnp.bfloat16)).astype(jnp.float32)
        softmax_low = lax.optimization_barrier(softmax.astype(jnp.bfloat16)).astype(jnp.float32)
        query_grad = jnp.einsum('hqk,kd->qhd', grad_scores, key_window) * score_scale
        key_grad = jnp.einsum('hqk,qhd->kd', grad_scores, query_tile) * score_scale
        value_grad = jnp.einsum('hqk,qhd->kd', softmax_low, grad_tile)
        key_acc = lax.dynamic_update_slice_in_dim(key_acc, lax.dynamic_slice_in_dim(key_acc, lowest, window, 0) + key_grad, lowest, 0)
        value_acc = lax.dynamic_update_slice_in_dim(value_acc, lax.dynamic_slice_in_dim(value_acc, lowest, window, 0) + value_grad, lowest, 0)
        return ((key_acc, value_acc), query_grad.reshape(BLOCK, HQ * HD))
    start_state = (jnp.zeros((LENGTH, HD), jnp.float32), jnp.zeros((LENGTH, HD), jnp.float32))
    (key_acc, value_acc), query_blocks = lax.scan(one_block, start_state, jnp.arange(2 * N_CTX, dtype=jnp.int32))
    query_all = query_blocks.reshape(LENGTH, HQ * HD)
    return (query_all[position].astype(jnp.bfloat16), key_acc[position].astype(jnp.bfloat16), value_acc[position].astype(jnp.bfloat16))

def reference(queries, keys, values, out_grad, doc_lengths, assignment):

    def per_section(section):
        return section_backward(queries[section], keys[section], values[section], out_grad[section], doc_lengths[section], assignment[section])
    query_grad, key_grad, value_grad = lax.map(per_section, jnp.arange(SECTIONS, dtype=jnp.int32))
    return (jnp.roll(query_grad, -1, axis=0), jnp.roll(key_grad, -1, axis=0), jnp.roll(value_grad, -1, axis=0))
```

```python
import functools
import math

import jax
import jax.numpy as jnp
from jax import lax
from jax.experimental import pallas as pl
from jax.experimental.pallas import tpu as pltpu
from jax.sharding import PartitionSpec as P

BLK = 256
HD = 128
WINDOW = 17
GROUP = 2
FAR = 262144.0
EXP_SCALE = math.log2(math.e) / math.sqrt(HD)
SCALE = 1.0 / math.sqrt(HD)


def attention_kernel(
    table, *refs, blocks, heads, chips
):
    q_own, q_par, g_own, g_par, key_mask, query_mask = refs[:6]
    pieces = refs[6 : 6 + 2 * chips]
    outs = refs[6 + 2 * chips : 6 + 4 * chips]
    dq_own, dq_par = refs[6 + 4 * chips : 8 + 4 * chips]
    (kv, kt, dk, dv, q, g, dq, qa, gt, ebuf, dbuf, mbuf, dqt, sem, osem) = refs[8 + 4 * chips :]
    nblk = kv.shape[0]
    half = blocks // 2
    core = table[0]
    qblk, first, src, dst = 1, 1 + blocks, 1 + 2 * blocks, 1 + 2 * blocks + 2 * chips

    copies = []
    for i in range(2 * chips):
        at = table[src + i]
        copies.append(pltpu.make_async_copy(pieces[i].at[pl.ds(0, BLK)], kv.at[at], sem.at[0]))
        copies.append(
            pltpu.make_async_copy(pieces[i].at[pl.ds(BLK, BLK)], kv.at[nblk - 1 - at], sem.at[0])
        )
    for local, (q_src, g_src) in enumerate(((q_own, g_own), (q_par, g_par))):
        for b in range(half):
            for h in range(heads):
                col = pl.multiple_of((core * heads + h) * HD, HD)
                for source, target in ((q_src, q), (g_src, g)):
                    copies.append(
                        pltpu.make_async_copy(
                            source.at[pl.ds(b * BLK, BLK), pl.ds(col, HD)],
                            target.at[local * half + b, h],
                            sem.at[0],
                        )
                    )
    for c in copies:
        c.start()
    dk[...] = jnp.zeros_like(dk)
    dv[...] = jnp.zeros_like(dv)
    for c in copies:
        c.wait()

    def turn(b, carry):
        kt[b] = kv[b, :, :HD].T
        return carry

    lax.fori_loop(0, nblk, turn, 0)

    def stats(hg, tile, slot, state, causal):
        m, l, d = state
        lhs = jnp.concatenate([kv[tile, :, :HD], key_mask[tile]], axis=1)
        s = jnp.dot(lhs, qa[hg], preferred_element_type=jnp.float32)
        if causal:
            key_at = lax.broadcasted_iota(jnp.int32, s.shape, 0)
            query_at = lax.broadcasted_iota(jnp.int32, s.shape, 1)
            s = jnp.where(key_at <= query_at, s, -FAR)
        dp = jnp.dot(kv[tile, :, HD:], gt[hg], preferred_element_type=jnp.float32)
        s = s.reshape(BLK // 8, 8, BLK)
        dp = dp.reshape(BLK // 8, 8, BLK)
        top = jnp.maximum(m, jnp.max(s, axis=0))
        e = jnp.exp2((s - top[None]) * EXP_SCALE)
        shrink = jnp.exp2((m - top) * EXP_SCALE)
        ebuf[hg, slot] = e
        dbuf[hg, slot] = dp
        mbuf[hg, slot] = top
        return (top, l * shrink + jnp.sum(e, axis=0), d * shrink + jnp.sum(e * dp, axis=0))

    def item(i, carry):
        n = i // (heads // GROUP)
        h0 = (i % (heads // GROUP)) * GROUP
        b = table[qblk + n]
        lo = table[first + n]
        last = b - lo
        for hg in range(GROUP):
            qa[hg, :HD] = q[n, h0 + hg].T
            qa[hg, HD:] = query_mask[n]
            gt[hg] = g[n, h0 + hg].T
        none = jnp.full((8, BLK), -FAR, jnp.float32)
        zero = jnp.zeros((8, BLK), jnp.float32)
        states = tuple(stats(hg, b, last, (none, zero, zero), True) for hg in range(GROUP))

        def forward(t, states):
            return tuple(stats(hg, lo + t, t, states[hg], False) for hg in range(GROUP))

        states = lax.fori_loop(0, last, forward, states)
        finals = []
        for hg in range(GROUP):
            m, l, d = states[hg]
            top = jnp.max(m, axis=0, keepdims=True)
            shrink = jnp.exp2((m - top) * EXP_SCALE)
            total = jnp.sum(l * shrink, axis=0, keepdims=True)
            inverse = 1.0 / total
            delta = jnp.sum(d * shrink, axis=0, keepdims=True) * inverse
            finals.append((top, inverse, delta))
        dqt[...] = jnp.zeros_like(dqt)

        def backward(t, carry):
            tile = lo + t
            probs, grads = [], []
            for hg in range(GROUP):
                top, inverse, delta = finals[hg]
                fix = jnp.exp2((mbuf[hg, t] - top) * EXP_SCALE) * inverse
                p = ebuf[hg, t] * fix[None]
                ds = p * (dbuf[hg, t] - delta[None])
                probs.append(p.reshape(BLK, BLK).astype(jnp.bfloat16))
                grads.append(ds.reshape(BLK, BLK).astype(jnp.bfloat16))
                dqt[hg] += jnp.dot(kt[tile], grads[hg], preferred_element_type=jnp.float32)
            g_rows = jnp.concatenate([g[n, h0 + hg] for hg in range(GROUP)], axis=0)
            q_rows = jnp.concatenate([q[n, h0 + hg] for hg in range(GROUP)], axis=0)
            dv[tile] += jnp.dot(
                jnp.concatenate(probs, axis=1), g_rows, preferred_element_type=jnp.float32
            )
            dk[tile] += jnp.dot(
                jnp.concatenate(grads, axis=1), q_rows, preferred_element_type=jnp.float32
            )
            return carry

        lax.fori_loop(0, last + 1, backward, 0)
        for hg in range(GROUP):
            dq[n, h0 + hg] = (dqt[hg] * SCALE).T.astype(jnp.bfloat16)
        return carry

    lax.fori_loop(0, blocks * heads // GROUP, item, 0)

    back = []
    for local, target in enumerate((dq_own, dq_par)):
        for b in range(half):
            for h in range(heads):
                back.append(
                    pltpu.make_async_copy(
                        dq.at[local * half + b, h],
                        target.at[pl.ds(b * BLK, BLK), pl.ds(h * HD, HD)],
                        osem.at[0],
                    )
                )
    for c in back:
        c.start()
    for i in range(2 * chips):
        at = table[dst + i]
        for row, block in ((0, at), (BLK, nblk - 1 - at)):
            outs[i][pl.ds(row, BLK), :HD] = (dk[block] * SCALE).astype(jnp.bfloat16)
            outs[i][pl.ds(row, BLK), HD:] = dv[block].astype(jnp.bfloat16)
    for c in back:
        c.wait()


def run_attention(table, q_own, q_par, g_own, g_par, key_mask, query_mask, pieces):
    blocks, heads = query_mask.shape[0], q_own.shape[1] // HD // 2
    chips = len(pieces) // 2
    rows = q_own.shape[0]
    nblk = key_mask.shape[0]
    hbm = pl.BlockSpec(memory_space=pl.ANY)
    vmem = pl.BlockSpec(memory_space=pltpu.VMEM)
    bf16, f32 = jnp.bfloat16, jnp.float32
    part = jax.ShapeDtypeStruct((rows, 2 * HD), bf16)
    grad = jax.ShapeDtypeStruct((rows, heads * HD), bf16)
    return pl.pallas_call(
        functools.partial(attention_kernel, blocks=blocks, heads=heads, chips=chips),
        out_shape=[part] * (2 * chips) + [grad] * 2,
        in_specs=[pl.BlockSpec(memory_space=pltpu.SMEM)]
        + [hbm] * 4
        + [vmem] * 2
        + [hbm] * (2 * chips),
        out_specs=[vmem] * (2 * chips) + [hbm] * 2,
        scratch_shapes=[
            pltpu.VMEM((nblk, BLK, 2 * HD), bf16),
            pltpu.VMEM((nblk, HD, BLK), bf16),
            pltpu.VMEM((nblk, BLK, HD), f32),
            pltpu.VMEM((nblk, BLK, HD), f32),
            pltpu.VMEM((blocks, heads, BLK, HD), bf16),
            pltpu.VMEM((blocks, heads, BLK, HD), bf16),
            pltpu.VMEM((blocks, heads, BLK, HD), bf16),
            pltpu.VMEM((GROUP, 2 * HD, BLK), bf16),
            pltpu.VMEM((GROUP, HD, BLK), bf16),
            pltpu.VMEM((GROUP, WINDOW, BLK // 8, 8, BLK), f32),
            pltpu.VMEM((GROUP, WINDOW, BLK // 8, 8, BLK), f32),
            pltpu.VMEM((GROUP, WINDOW, 8, BLK), f32),
            pltpu.VMEM((GROUP, HD, BLK), f32),
            pltpu.SemaphoreType.DMA((1,)),
            pltpu.SemaphoreType.DMA((1,)),
        ],
        compiler_params=pltpu.CompilerParams(vmem_limit_bytes=60 * 1024 * 1024),
        name="attention",
    )(table, q_own, q_par, g_own, g_par, key_mask, query_mask, *pieces)


def masks_of(doc_sizes, query_blocks, nblk):
    ends = jnp.cumsum(doc_sizes)
    starts = ends - doc_sizes
    pad = HD - doc_sizes.shape[0]
    never = nblk * BLK
    starts_wide = jnp.pad(starts, (0, pad), constant_values=never)
    ends_wide = jnp.pad(ends, (0, pad), constant_values=never)
    pos = jnp.arange(never, dtype=jnp.int32)[:, None]
    inside = (starts_wide[None, :] <= pos) & (pos < ends_wide[None, :])
    key_mask = jnp.where(inside, 0.0, 1.0).astype(jnp.bfloat16).reshape(nblk, BLK, HD)
    q_pos = query_blocks[:, None, None] * BLK + jnp.arange(BLK, dtype=jnp.int32)[None, None, :]
    q_inside = (starts_wide[None, :, None] <= q_pos) & (q_pos < ends_wide[None, :, None])
    query_mask = jnp.where(q_inside, -FAR, 0.0).astype(jnp.bfloat16)
    first_row = query_blocks * BLK
    reach = jnp.where(starts[None, :] <= first_row[:, None], starts[None, :], 0)
    first_tile = jnp.max(reach, axis=1) // BLK
    return key_mask, query_mask, first_tile


def local(queries, keys, values, out_grad, doc_lengths, assignment):
    n_ctx = lax.axis_size("ctx")
    n_pipe = lax.axis_size("pipe")
    nblk = 2 * n_ctx
    me = lax.axis_index("ctx")
    core = me % 2
    n_z = 4
    n_y = n_ctx // 2 // n_z
    offsets = [(dy, dz) for dy in range(n_y) for dz in range(n_z)]
    chips = len(offsets)

    def place(index, dy, dz, swap):
        y, z, c = index // (2 * n_z), index // 2 % n_z, index % 2
        return ((y + dy) % n_y) * 2 * n_z + ((z + dz) % n_z) * 2 + (1 - c if swap else c)

    def hop(x, dy, dz):
        if (dy, dz) == (0, 0):
            return x
        return lax.ppermute(x, "ctx", [(i, place(i, dy, dz, False)) for i in range(n_ctx)])

    def swap(x):
        return lax.ppermute(x, "ctx", [(i, i ^ 1) for i in range(n_ctx)])

    placing = assignment[0].astype(jnp.int32)
    q, g = queries[0], out_grad[0]
    packed = jnp.concatenate([keys[0], values[0]], axis=1)
    q_par, g_par = swap(q), swap(g)
    mine = [hop(packed, dy, dz) for dy, dz in offsets]
    others = [swap(x) for x in mine]

    own = placing[me]
    par = placing[me ^ 1]
    query_blocks = jnp.stack([own, nblk - 1 - own, par, nblk - 1 - par])
    key_mask, query_mask, first_tile = masks_of(doc_lengths[0], query_blocks, nblk)
    sources = jnp.stack(
        [place(me, -dy, -dz, s) for s in (False, True) for dy, dz in offsets]
    )
    targets = jnp.stack([place(me, dy, dz, s) for s in (False, True) for dy, dz in offsets])
    table = jnp.concatenate(
        [core[None], query_blocks, first_tile, placing[sources], placing[targets]]
    ).astype(jnp.int32)

    results = run_attention(
        table, q, q_par, g, g_par, key_mask, query_mask, mine + others
    )
    own_parts, par_parts = results[:chips], results[chips : 2 * chips]
    dq_own, dq_par = results[2 * chips :]

    def route(flip):
        pairs = []
        for s in range(n_pipe):
            for i in range(n_ctx):
                to = (s - 1) % n_pipe * n_ctx + (i ^ 1 if flip else i)
                pairs.append((s * n_ctx + i, to))
        return pairs

    dq_same = lax.ppermute(dq_own, ("pipe", "ctx"), route(False))
    dq_flip = lax.ppermute(dq_par, ("pipe", "ctx"), route(True))

    swapped = [swap(x) for x in par_parts]
    sums = [
        (a.astype(jnp.float32) + b.astype(jnp.float32)).astype(jnp.bfloat16)
        for a, b in zip(own_parts, swapped)
    ]
    arrived = [hop(x, dy, dz) for x, (dy, dz) in zip(sums, offsets)]
    kv_grad = functools.reduce(lambda a, b: a + b, [x.astype(jnp.float32) for x in arrived])
    kv_out = lax.ppermute(
        kv_grad.astype(jnp.bfloat16), "pipe", [((i + 1) % n_pipe, i) for i in range(n_pipe)]
    )
    width = dq_same.shape[1]
    left = jnp.where(core == 0, dq_same, dq_flip)
    right = jnp.where(core == 0, dq_flip, dq_same)
    q_out = jnp.concatenate([left, right], axis=1)
    return (q_out[None], kv_out[:, :HD][None], kv_out[:, HD:][None])


def solution(mesh):
    return jax.shard_map(
        local,
        mesh=mesh,
        in_specs=(
            P("pipe", "ctx", None),
            P("pipe", "ctx", None),
            P("pipe", "ctx", None),
            P("pipe", "ctx", None),
            P("pipe", None),
            P("pipe", None),
        ),
        out_specs=(P("pipe", "ctx", None), P("pipe", "ctx", None), P("pipe", "ctx", None)),
        check_vma=False,
    )
```

```python
import functools
import math

import jax
import jax.numpy as jnp
from jax import lax
from jax.experimental import pallas as pl
from jax.experimental.pallas import tpu as pltpu
from jax.sharding import PartitionSpec as P

BLK = 256
HD = 128
WINDOW = 17
N_Z = 4
CHUNKS = 2
FAR = 262144.0
EXP_SCALE = math.log2(math.e) / math.sqrt(HD)
SCALE = 1.0 / math.sqrt(HD)


def attention_kernel(
    docs, placing, where, *refs, blocks, heads, chips
):
    q_own, q_par, g_own, g_par = refs[:4]
    pieces = refs[4 : 4 + 2 * chips]
    refs = refs[4 + 2 * chips :]
    own_outs, par_outs, dq_own, dq_par = refs[:chips], refs[chips : chips + 2], *refs[chips + 2 : chips + 4]
    (kv, key_mask, kt, dk, dv, q, g, dq, dqt, even, odd, sem, osem) = refs[chips + 4 :]
    nblk = kv.shape[0]
    half = blocks // 2
    items = blocks * heads
    me = where[0]
    core = lax.rem(me, 2)

    def chip_at(sign, r, swap):
        dy, dz = r // N_Z, r % N_Z
        y = lax.rem(me // (2 * N_Z) + dy, chips // N_Z)
        z = lax.rem(lax.rem(me // 2, N_Z) + sign * dz + N_Z, N_Z)
        return placing[y * 2 * N_Z + z * 2 + (1 - core if swap else core)]

    copies = []
    for i in range(2 * chips):
        at = chip_at(-1, i % chips, i >= chips)
        copies.append(pltpu.make_async_copy(pieces[i].at[pl.ds(0, BLK)], kv.at[at], sem.at[0]))
        copies.append(
            pltpu.make_async_copy(pieces[i].at[pl.ds(BLK, BLK)], kv.at[nblk - 1 - at], sem.at[0])
        )
    for local, (q_src, g_src) in enumerate(((q_own, g_own), (q_par, g_par))):
        for b in range(half):
            for h in range(heads):
                col = pl.multiple_of((core * heads + h) * HD, HD)
                for source, target in ((q_src, q), (g_src, g)):
                    copies.append(
                        pltpu.make_async_copy(
                            source.at[pl.ds(b * BLK, BLK), pl.ds(col, HD)],
                            target.at[local * half + b, h],
                            sem.at[0],
                        )
                    )
    for c in copies:
        c.start()

    own, par = placing[me], placing[me + 1 - 2 * core]
    query_blocks = [own, nblk - 1 - own, par, nblk - 1 - par]
    starts, ends = [], []
    at = jnp.int32(0)
    for i in range(docs.shape[0]):
        starts.append(at)
        at = at + docs[i]
        ends.append(at)
    firsts = []
    for b in query_blocks:
        reach = jnp.int32(0)
        for x in starts:
            reach = jnp.where(x <= b * BLK, x, reach)
        firsts.append(reach // BLK)
    lane = lax.broadcasted_iota(jnp.int32, (BLK, HD), 1)
    row = lax.broadcasted_iota(jnp.int32, (BLK, HD), 0)
    lane_start = jnp.full((BLK, HD), nblk * BLK, jnp.int32)
    lane_end = lane_start
    for i in range(docs.shape[0]):
        lane_start = jnp.where(lane == i, starts[i], lane_start)
        lane_end = jnp.where(lane == i, ends[i], lane_end)
    lane_start, lane_end = lane_start - row, lane_end - row

    def inside(b):
        return (lane_start <= b * BLK) & (b * BLK < lane_end)

    def clear(b, carry):
        dk[b] = jnp.zeros(dk.shape[1:], dk.dtype)
        dv[b] = jnp.zeros(dv.shape[1:], dv.dtype)
        key_mask[b] = jnp.where(inside(b), 0.0, 1.0).astype(jnp.bfloat16)
        return carry

    lax.fori_loop(0, nblk, clear, 0)
    for c in copies:
        c.wait()

    def turn(b, carry):
        used = False
        for top, low in zip(query_blocks, firsts):
            used = used | ((b <= top) & (b >= low))

        @pl.when(used)
        def _():
            kt[b] = kv[b, :, :HD].T

        return carry

    lax.fori_loop(0, nblk, turn, 0)

    def choose(n, options):
        out = options[-1]
        for i in range(len(options) - 1):
            out = jnp.where(n == i, options[i], out)
        return out

    def span(i):
        n = i // heads
        b, lo = choose(n, query_blocks), choose(n, firsts)
        return b, lo, b - lo

    def prepare(i, b, bufs):
        qa, gt = bufs[:2]
        n, h = i // heads, lax.rem(i, heads)
        qa[:HD] = q[n, h].T
        qa[HD:] = jnp.where(inside(b), -FAR, 0.0).astype(jnp.bfloat16).T
        gt[...] = g[n, h].T

    def stats(tile, slot, bufs, state, causal, size):
        qa, gt, ebuf, dbuf, mbuf = bufs
        m, l, d = state
        rows = size * BLK
        kvs = kv[pl.ds(tile, size)].reshape(rows, 2 * HD)
        lhs = jnp.concatenate([kvs[:, :HD], key_mask[pl.ds(tile, size)].reshape(rows, HD)], axis=1)
        s = jnp.dot(lhs, qa[...], preferred_element_type=jnp.float32)
        if causal:
            key_at = lax.broadcasted_iota(jnp.int32, s.shape, 0)
            query_at = lax.broadcasted_iota(jnp.int32, s.shape, 1)
            s = jnp.where(key_at <= query_at, s, -FAR)
        dp = jnp.dot(kvs[:, HD:], gt[...], preferred_element_type=jnp.float32)
        step = BLK // 8 // CHUNKS
        s = s.reshape(size * CHUNKS, step, 8, BLK)
        dp = dp.reshape(size * CHUNKS, step, 8, BLK)
        for c in range(size * CHUNKS):
            at, part = slot + c // CHUNKS, pl.ds(c % CHUNKS * step, step)
            sc, dpc = s[c], dp[c]
            top = jnp.maximum(m, jnp.max(sc, axis=0))
            e = jnp.exp2((sc - top[None]) * EXP_SCALE)
            shrink = jnp.exp2((m - top) * EXP_SCALE)
            ebuf[at, part] = e
            dbuf[at, part] = dpc
            mbuf[at, c % CHUNKS] = top
            m, l, d = (
                top,
                l * shrink + jnp.sum(e, axis=0),
                d * shrink + jnp.sum(e * dpc, axis=0),
            )
        return (m, l, d)

    def grads(tile, slot, bufs, n, h, final, size):
        _, _, ebuf, dbuf, mbuf = bufs
        top, inverse, delta = final
        step = BLK // 8 // CHUNKS
        probs, scores = [], []
        for c in range(size * CHUNKS):
            at, part = slot + c // CHUNKS, pl.ds(c % CHUNKS * step, step)
            fix = jnp.exp2((mbuf[at, c % CHUNKS] - top) * EXP_SCALE) * inverse
            p = ebuf[at, part] * fix[None]
            ds = p * (dbuf[at, part] - delta[None])
            probs.append(p.reshape(BLK // CHUNKS, BLK).astype(jnp.bfloat16))
            scores.append(ds.reshape(BLK // CHUNKS, BLK).astype(jnp.bfloat16))
        p = jnp.concatenate(probs, axis=0)
        ds = jnp.concatenate(scores, axis=0)
        keys_t = jnp.concatenate([kt[tile + i] for i in range(size)], axis=1)
        dqt[...] += jnp.dot(keys_t, ds, preferred_element_type=jnp.float32)
        shape = (size, BLK, HD)
        dv[pl.ds(tile, size)] += jnp.dot(
            p, g[n, h], preferred_element_type=jnp.float32
        ).reshape(shape)
        dk[pl.ds(tile, size)] += jnp.dot(
            ds, q[n, h], preferred_element_type=jnp.float32
        ).reshape(shape)

    def finish(state):
        m, l, d = state
        top = jnp.max(m, axis=0, keepdims=True)
        shrink = jnp.exp2((m - top) * EXP_SCALE)
        inverse = 1.0 / jnp.sum(l * shrink, axis=0, keepdims=True)
        delta = jnp.sum(d * shrink, axis=0, keepdims=True) * inverse
        return (top, inverse, delta)

    none = jnp.full((8, BLK), -FAR, jnp.float32)
    zero = jnp.zeros((8, BLK), jnp.float32)
    fresh = (none, zero, zero)

    def sweep(low, high, body, state):
        pairs = (high - low) // 2
        state = lax.fori_loop(0, pairs, lambda t, st: body(low + 2 * t, 2, st), state)
        return lax.fori_loop(low + 2 * pairs, high, lambda t, st: body(t, 1, st), state)

    def start():
        b, lo, count = span(0)
        prepare(0, b, even)
        state = stats(b, count, even, fresh, True, 1)

        def only(t, size, state):
            return stats(lo + t, t, even, state, False, size)

        return finish(sweep(0, count, only, state))

    def step(i, final, now, later):
        n, h = i // heads, lax.rem(i, heads)
        nxt = jnp.minimum(i + 1, items - 1)
        b, lo, count = span(i)
        b_n, lo_n, count_n = span(nxt)
        todo = jnp.where(i + 1 < items, count_n, 0)
        both = jnp.minimum(count, todo) // 2
        prepare(nxt, b_n, later)
        dqt[...] = jnp.zeros_like(dqt)
        state = stats(b_n, count_n, later, fresh, True, 1)
        grads(b, count, now, n, h, final, 1)

        def joint(t, state):
            state = stats(lo_n + 2 * t, 2 * t, later, state, False, 2)
            grads(lo + 2 * t, 2 * t, now, n, h, final, 2)
            return state

        def ahead(t, size, state):
            return stats(lo_n + t, t, later, state, False, size)

        def behind(t, size, carry):
            grads(lo + t, t, now, n, h, final, size)
            return carry

        state = lax.fori_loop(0, both, joint, state)
        state = sweep(2 * both, todo, ahead, state)
        sweep(2 * both, count, behind, 0)
        dq[n, h] = (dqt[...] * SCALE).T.astype(jnp.bfloat16)
        return finish(state)

    def pair(j, final):
        final = step(2 * j, final, even, odd)
        return step(2 * j + 1, final, odd, even)

    lax.fori_loop(0, items // 2, pair, start())

    back = []
    for local, target in enumerate((dq_own, dq_par)):
        for b in range(half):
            for h in range(heads):
                back.append(
                    pltpu.make_async_copy(
                        dq.at[local * half + b, h],
                        target.at[pl.ds(b * BLK, BLK), pl.ds(h * HD, HD)],
                        osem.at[0],
                    )
                )
    for c in back:
        c.start()
    for i in range(2 * chips):
        at = chip_at(1, i % chips, i >= chips)
        out = own_outs[i] if i < chips else par_outs[(i - chips) // N_Z].at[i % N_Z]
        for first_row, block in ((0, at), (BLK, nblk - 1 - at)):
            out[pl.ds(first_row, BLK), :HD] = (dk[block] * SCALE).astype(jnp.bfloat16)
            out[pl.ds(first_row, BLK), HD:] = dv[block].astype(jnp.bfloat16)
    for c in back:
        c.wait()


def run_attention(docs, placing, where, q_own, q_par, g_own, g_par, pieces):
    chips = len(pieces) // 2
    heads = q_own.shape[1] // HD // 2
    rows = q_own.shape[0]
    blocks, nblk = 2 * rows // BLK, 4 * chips
    hbm = pl.BlockSpec(memory_space=pltpu.HBM)
    vmem = pl.BlockSpec(memory_space=pltpu.VMEM)
    smem = pl.BlockSpec(memory_space=pltpu.SMEM)
    bf16, f32 = jnp.bfloat16, jnp.float32
    part = jax.ShapeDtypeStruct((rows, 2 * HD), bf16)
    parts = jax.ShapeDtypeStruct((N_Z, rows, 2 * HD), bf16)
    grad = jax.ShapeDtypeStruct((rows, heads * HD), bf16)
    work = (
        pltpu.VMEM((2 * HD, BLK), bf16),
        pltpu.VMEM((HD, BLK), bf16),
        pltpu.VMEM((WINDOW, BLK // 8, 8, BLK), f32),
        pltpu.VMEM((WINDOW, BLK // 8, 8, BLK), f32),
        pltpu.VMEM((WINDOW, CHUNKS, 8, BLK), f32),
    )
    return pl.pallas_call(
        functools.partial(attention_kernel, blocks=blocks, heads=heads, chips=chips),
        out_shape=[part] * chips + [parts] * (chips // N_Z) + [grad] * 2,
        in_specs=[smem] * 3 + [hbm] * (4 + 2 * chips),
        out_specs=[vmem] * (chips + chips // N_Z) + [hbm] * 2,
        scratch_shapes=[
            pltpu.VMEM((nblk, BLK, 2 * HD), bf16),
            pltpu.VMEM((nblk, BLK, HD), bf16),
            pltpu.VMEM((nblk, HD, BLK), bf16),
            pltpu.VMEM((nblk, BLK, HD), f32),
            pltpu.VMEM((nblk, BLK, HD), f32),
            pltpu.VMEM((blocks, heads, BLK, HD), bf16),
            pltpu.VMEM((blocks, heads, BLK, HD), bf16),
            pltpu.VMEM((blocks, heads, BLK, HD), bf16),
            pltpu.VMEM((HD, BLK), f32),
            work,
            work,
            pltpu.SemaphoreType.DMA((1,)),
            pltpu.SemaphoreType.DMA((1,)),
        ],
        compiler_params=pltpu.CompilerParams(vmem_limit_bytes=58 * 1024 * 1024),
        name="attention",
    )(docs, placing, where, q_own, q_par, g_own, g_par, *pieces)


def local(queries, keys, values, out_grad, doc_lengths, assignment):
    n_ctx = lax.axis_size("ctx")
    n_pipe = lax.axis_size("pipe")
    me = lax.axis_index("ctx")
    core = me % 2
    n_y = n_ctx // 2 // N_Z

    def hop(x, dy, dz):
        def to(i):
            y, z, c = i // (2 * N_Z), i // 2 % N_Z, i % 2
            return ((y + dy) % n_y) * 2 * N_Z + ((z + dz) % N_Z) * 2 + c

        return lax.ppermute(x, "ctx", [(i, to(i)) for i in range(n_ctx)])

    def swap(x):
        return lax.ppermute(x, "ctx", [(i, i ^ 1) for i in range(n_ctx)])

    turns = list(range(1, N_Z))
    q, g = queries[0], out_grad[0]
    packed = jnp.concatenate([keys[0], values[0]], axis=1)
    facing = hop(packed, 1, 0)
    mine = [packed] + [hop(packed, 0, dz) for dz in turns]
    mine += [facing] + [hop(facing, 0, dz) for dz in turns]
    q_par, g_par = swap(q), swap(g)
    others = [swap(x) for x in mine]

    results = run_attention(
        doc_lengths[0].astype(jnp.int32),
        assignment[0].astype(jnp.int32),
        me[None].astype(jnp.int32),
        q,
        q_par,
        g,
        g_par,
        mine + others,
    )
    chips = len(mine)
    own_parts, par_parts = results[:chips], results[chips : chips + n_y]
    dq_own, dq_par = results[chips + n_y :]

    def route(flip):
        pairs = []
        for s in range(n_pipe):
            for i in range(n_ctx):
                to = (s - 1) % n_pipe * n_ctx + (i ^ 1 if flip else i)
                pairs.append((s * n_ctx + i, to))
        return pairs

    def total(parts):
        return functools.reduce(lambda a, b: a + b, [x.astype(jnp.float32) for x in parts])

    far_swap, near_swap = swap(par_parts[1]), swap(par_parts[0])
    dq_same = lax.ppermute(dq_own, ("pipe", "ctx"), route(False))
    dq_flip = lax.ppermute(dq_par, ("pipe", "ctx"), route(True))
    far = [
        total([own_parts[N_Z + i], far_swap[i]]).astype(jnp.bfloat16) for i in range(N_Z)
    ]
    far_in = [hop(far[dz], 0, dz) for dz in turns]
    near = [total([own_parts[i], near_swap[i]]).astype(jnp.bfloat16) for i in range(N_Z)]
    near_in = [hop(near[dz], 0, dz) for dz in turns]
    crossed = hop(total([far[0]] + far_in).astype(jnp.bfloat16), 1, 0)
    kv_grad = total([near[0]] + near_in + [crossed])
    kv_out = lax.ppermute(
        kv_grad.astype(jnp.bfloat16), "pipe", [((i + 1) % n_pipe, i) for i in range(n_pipe)]
    )
    left = jnp.where(core == 0, dq_same, dq_flip)
    right = jnp.where(core == 0, dq_flip, dq_same)
    q_out = jnp.concatenate([left, right], axis=1)
    return (q_out[None], kv_out[:, :HD][None], kv_out[:, HD:][None])


def solution(mesh):
    return jax.shard_map(
        local,
        mesh=mesh,
        in_specs=(
            P("pipe", "ctx", None),
            P("pipe", "ctx", None),
            P("pipe", "ctx", None),
            P("pipe", "ctx", None),
            P("pipe", None),
            P("pipe", None),
        ),
        out_specs=(P("pipe", "ctx", None), P("pipe", "ctx", None), P("pipe", "ctx", None)),
        check_vma=False,
    )
```

```python
import functools
import math

import jax
import jax.numpy as jnp
from jax import lax
from jax.experimental import pallas as pl
from jax.experimental.pallas import tpu as pltpu
from jax.sharding import PartitionSpec as P


BLK = 256
HD = 128
WINDOW = 17
N_Z = 4
CHUNKS = 2
FAR = 262144.0
EXP_SCALE = math.log2(math.e) / math.sqrt(HD)
SCALE = 1.0 / math.sqrt(HD)


def attention_kernel(
    docs, placing, where, *refs, blocks, heads, chips
):
    q_own, q_par, g_own, g_par = refs[:4]
    pieces = refs[4 : 4 + 2 * chips]
    refs = refs[4 + 2 * chips :]
    own_outs, par_outs, dq_own, dq_par = refs[:chips], refs[chips : chips + 2], *refs[chips + 2 : chips + 4]
    (kv, key_mask, kt, dk, dv, q, g, dq, dqt, even, odd, sem, osem) = refs[chips + 4 :]
    nblk = kv.shape[0]
    half = blocks // 2
    items = blocks * heads
    me = where[0]
    core = lax.rem(me, 2)

    def chip_at(sign, r, swap):
        dy, dz = r // N_Z, r % N_Z
        y = lax.rem(me // (2 * N_Z) + dy, chips // N_Z)
        z = lax.rem(lax.rem(me // 2, N_Z) + sign * dz + N_Z, N_Z)
        return placing[y * 2 * N_Z + z * 2 + (1 - core if swap else core)]

    copies = []
    for i in range(2 * chips):
        at = chip_at(-1, i % chips, i >= chips)
        copies.append(pltpu.make_async_copy(pieces[i].at[pl.ds(0, BLK)], kv.at[at], sem.at[0]))
        copies.append(
            pltpu.make_async_copy(pieces[i].at[pl.ds(BLK, BLK)], kv.at[nblk - 1 - at], sem.at[0])
        )
    for local, (q_src, g_src) in enumerate(((q_own, g_own), (q_par, g_par))):
        for b in range(half):
            for h in range(heads):
                col = pl.multiple_of((core * heads + h) * HD, HD)
                for source, target in ((q_src, q), (g_src, g)):
                    copies.append(
                        pltpu.make_async_copy(
                            source.at[pl.ds(b * BLK, BLK), pl.ds(col, HD)],
                            target.at[local * half + b, h],
                            sem.at[0],
                        )
                    )
    for c in copies:
        c.start()

    own, par = placing[me], placing[me + 1 - 2 * core]
    query_blocks = [own, nblk - 1 - own, par, nblk - 1 - par]
    starts, ends = [], []
    at = jnp.int32(0)
    for i in range(docs.shape[0]):
        starts.append(at)
        at = at + docs[i]
        ends.append(at)
    firsts = []
    for b in query_blocks:
        reach = jnp.int32(0)
        for x in starts:
            reach = jnp.where(x <= b * BLK, x, reach)
        firsts.append(reach // BLK)
    lane = lax.broadcasted_iota(jnp.int32, (BLK, HD), 1)
    row = lax.broadcasted_iota(jnp.int32, (BLK, HD), 0)
    lane_start = jnp.full((BLK, HD), nblk * BLK, jnp.int32)
    lane_end = lane_start
    for i in range(docs.shape[0]):
        lane_start = jnp.where(lane == i, starts[i], lane_start)
        lane_end = jnp.where(lane == i, ends[i], lane_end)
    lane_start, lane_end = lane_start - row, lane_end - row

    def inside(b):
        return (lane_start <= b * BLK) & (b * BLK < lane_end)

    def clear(b, carry):
        dk[b] = jnp.zeros(dk.shape[1:], dk.dtype)
        dv[b] = jnp.zeros(dv.shape[1:], dv.dtype)
        key_mask[b] = jnp.where(inside(b), 0.0, 1.0).astype(jnp.bfloat16)
        return carry

    lax.fori_loop(0, nblk, clear, 0)
    for c in copies:
        c.wait()

    def turn(b, carry):
        used = False
        for top, low in zip(query_blocks, firsts):
            used = used | ((b <= top) & (b >= low))

        @pl.when(used)
        def _():
            kt[b] = kv[b, :, :HD].T

        return carry

    lax.fori_loop(0, nblk, turn, 0)

    def choose(n, options):
        out = options[-1]
        for i in range(len(options) - 1):
            out = jnp.where(n == i, options[i], out)
        return out

    def span(i):
        n = i // heads
        b, lo = choose(n, query_blocks), choose(n, firsts)
        return b, lo, b - lo

    def prepare(i, b, bufs):
        qa, gt = bufs[:2]
        n, h = i // heads, lax.rem(i, heads)
        qa[:HD] = q[n, h].T
        qa[HD:] = jnp.where(inside(b), -FAR, 0.0).astype(jnp.bfloat16).T
        gt[...] = g[n, h].T

    def stats(tile, slot, bufs, state, causal, size):
        qa, gt, ebuf, dbuf, mbuf = bufs
        m, l, d = state
        rows = size * BLK
        kvs = kv[pl.ds(tile, size)].reshape(rows, 2 * HD)
        lhs = jnp.concatenate([kvs[:, :HD], key_mask[pl.ds(tile, size)].reshape(rows, HD)], axis=1)
        s = jnp.dot(lhs, qa[...], preferred_element_type=jnp.float32)
        if causal:
            key_at = lax.broadcasted_iota(jnp.int32, s.shape, 0)
            query_at = lax.broadcasted_iota(jnp.int32, s.shape, 1)
            s = jnp.where(key_at <= query_at, s, -FAR)
        dp = jnp.dot(kvs[:, HD:], gt[...], preferred_element_type=jnp.float32)
        step = BLK // 8 // CHUNKS
        s = s.reshape(size * CHUNKS, step, 8, BLK)
        dp = dp.reshape(size * CHUNKS, step, 8, BLK)
        for c in range(size * CHUNKS):
            at, part = slot + c // CHUNKS, pl.ds(c % CHUNKS * step, step)
            sc, dpc = s[c], dp[c]
            top = jnp.maximum(m, jnp.max(sc, axis=0))
            e = jnp.exp2((sc - top[None]) * EXP_SCALE)
            shrink = jnp.exp2((m - top) * EXP_SCALE)
            ebuf[at, part] = e
            dbuf[at, part] = dpc
            mbuf[at, c % CHUNKS] = top
            m, l, d = (
                top,
                l * shrink + jnp.sum(e, axis=0),
                d * shrink + jnp.sum(e * dpc, axis=0),
            )
        return (m, l, d)

    def grads(tile, slot, bufs, n, h, final, size):
        _, _, ebuf, dbuf, mbuf = bufs
        top, inverse, delta = final
        step = BLK // 8 // CHUNKS
        probs, scores = [], []
        for c in range(size * CHUNKS):
            at, part = slot + c // CHUNKS, pl.ds(c % CHUNKS * step, step)
            fix = jnp.exp2((mbuf[at, c % CHUNKS] - top) * EXP_SCALE) * inverse
            p = ebuf[at, part] * fix[None]
            ds = p * (dbuf[at, part] - delta[None])
            probs.append(p.reshape(BLK // CHUNKS, BLK).astype(jnp.bfloat16))
            scores.append(ds.reshape(BLK // CHUNKS, BLK).astype(jnp.bfloat16))
        p = jnp.concatenate(probs, axis=0)
        ds = jnp.concatenate(scores, axis=0)
        keys_t = jnp.concatenate([kt[tile + i] for i in range(size)], axis=1)
        dqt[...] += jnp.dot(keys_t, ds, preferred_element_type=jnp.float32)
        shape = (size, BLK, HD)
        dv[pl.ds(tile, size)] += jnp.dot(
            p, g[n, h], preferred_element_type=jnp.float32
        ).reshape(shape)
        dk[pl.ds(tile, size)] += jnp.dot(
            ds, q[n, h], preferred_element_type=jnp.float32
        ).reshape(shape)

    def finish(state):
        m, l, d = state
        top = jnp.max(m, axis=0, keepdims=True)
        shrink = jnp.exp2((m - top) * EXP_SCALE)
        inverse = 1.0 / jnp.sum(l * shrink, axis=0, keepdims=True)
        delta = jnp.sum(d * shrink, axis=0, keepdims=True) * inverse
        return (top, inverse, delta)

    none = jnp.full((8, BLK), -FAR, jnp.float32)
    zero = jnp.zeros((8, BLK), jnp.float32)
    fresh = (none, zero, zero)

    def sweep(low, high, body, state):
        pairs = (high - low) // 2
        state = lax.fori_loop(0, pairs, lambda t, st: body(low + 2 * t, 2, st), state)
        return lax.fori_loop(low + 2 * pairs, high, lambda t, st: body(t, 1, st), state)

    def start():
        b, lo, count = span(0)
        prepare(0, b, even)
        state = stats(b, count, even, fresh, True, 1)

        def only(t, size, state):
            return stats(lo + t, t, even, state, False, size)

        return finish(sweep(0, count, only, state))

    def step(i, final, now, later):
        n, h = i // heads, lax.rem(i, heads)
        nxt = jnp.minimum(i + 1, items - 1)
        b, lo, count = span(i)
        b_n, lo_n, count_n = span(nxt)
        todo = jnp.where(i + 1 < items, count_n, 0)
        both = jnp.minimum(count, todo) // 2
        prepare(nxt, b_n, later)
        dqt[...] = jnp.zeros_like(dqt)
        state = stats(b_n, count_n, later, fresh, True, 1)
        grads(b, count, now, n, h, final, 1)

        def joint(t, state):
            state = stats(lo_n + 2 * t, 2 * t, later, state, False, 2)
            grads(lo + 2 * t, 2 * t, now, n, h, final, 2)
            return state

        def ahead(t, size, state):
            return stats(lo_n + t, t, later, state, False, size)

        def behind(t, size, carry):
            grads(lo + t, t, now, n, h, final, size)
            return carry

        state = lax.fori_loop(0, both, joint, state)
        state = sweep(2 * both, todo, ahead, state)
        sweep(2 * both, count, behind, 0)
        dq[n, h] = (dqt[...] * SCALE).T.astype(jnp.bfloat16)
        return finish(state)

    def pair(j, final):
        final = step(2 * j, final, even, odd)
        return step(2 * j + 1, final, odd, even)

    lax.fori_loop(0, items // 2, pair, start())

    back = []
    for local, target in enumerate((dq_own, dq_par)):
        for b in range(half):
            for h in range(heads):
                back.append(
                    pltpu.make_async_copy(
                        dq.at[local * half + b, h],
                        target.at[pl.ds(b * BLK, BLK), pl.ds(h * HD, HD)],
                        osem.at[0],
                    )
                )
    for c in back:
        c.start()
    for i in range(2 * chips):
        at = chip_at(1, i % chips, i >= chips)
        out = own_outs[i] if i < chips else par_outs[(i - chips) // N_Z].at[i % N_Z]
        for first_row, block in ((0, at), (BLK, nblk - 1 - at)):
            out[pl.ds(first_row, BLK), :HD] = (dk[block] * SCALE).astype(jnp.bfloat16)
            out[pl.ds(first_row, BLK), HD:] = dv[block].astype(jnp.bfloat16)
    for c in back:
        c.wait()


def run_attention(docs, placing, where, q_own, q_par, g_own, g_par, pieces):
    chips = len(pieces) // 2
    heads = q_own.shape[1] // HD // 2
    rows = q_own.shape[0]
    blocks, nblk = 2 * rows // BLK, 4 * chips
    hbm = pl.BlockSpec(memory_space=pltpu.HBM)
    vmem = pl.BlockSpec(memory_space=pltpu.VMEM)
    smem = pl.BlockSpec(memory_space=pltpu.SMEM)
    bf16, f32 = jnp.bfloat16, jnp.float32
    part = jax.ShapeDtypeStruct((rows, 2 * HD), bf16)
    parts = jax.ShapeDtypeStruct((N_Z, rows, 2 * HD), bf16)
    grad = jax.ShapeDtypeStruct((rows, heads * HD), bf16)
    work = (
        pltpu.VMEM((2 * HD, BLK), bf16),
        pltpu.VMEM((HD, BLK), bf16),
        pltpu.VMEM((WINDOW, BLK // 8, 8, BLK), f32),
        pltpu.VMEM((WINDOW, BLK // 8, 8, BLK), f32),
        pltpu.VMEM((WINDOW, CHUNKS, 8, BLK), f32),
    )
    return pl.pallas_call(
        functools.partial(attention_kernel, blocks=blocks, heads=heads, chips=chips),
        out_shape=[part] * chips + [parts] * (chips // N_Z) + [grad] * 2,
        in_specs=[smem] * 3 + [hbm] * (4 + 2 * chips),
        out_specs=[vmem] * (chips + chips // N_Z) + [hbm] * 2,
        scratch_shapes=[
            pltpu.VMEM((nblk, BLK, 2 * HD), bf16),
            pltpu.VMEM((nblk, BLK, HD), bf16),
            pltpu.VMEM((nblk, HD, BLK), bf16),
            pltpu.VMEM((nblk, BLK, HD), f32),
            pltpu.VMEM((nblk, BLK, HD), f32),
            pltpu.VMEM((blocks, heads, BLK, HD), bf16),
            pltpu.VMEM((blocks, heads, BLK, HD), bf16),
            pltpu.VMEM((blocks, heads, BLK, HD), bf16),
            pltpu.VMEM((HD, BLK), f32),
            work,
            work,
            pltpu.SemaphoreType.DMA((1,)),
            pltpu.SemaphoreType.DMA((1,)),
        ],
        compiler_params=pltpu.CompilerParams(vmem_limit_bytes=58 * 1024 * 1024),
        name="attention",
    )(docs, placing, where, q_own, q_par, g_own, g_par, *pieces)


def local(queries, keys, values, out_grad, doc_lengths, assignment):
    n_ctx = lax.axis_size("ctx")
    n_pipe = lax.axis_size("pipe")
    me = lax.axis_index("ctx")
    core = me % 2
    n_y = n_ctx // 2 // N_Z

    def hop(x, dy, dz):
        def to(i):
            y, z, c = i // (2 * N_Z), i // 2 % N_Z, i % 2
            return ((y + dy) % n_y) * 2 * N_Z + ((z + dz) % N_Z) * 2 + c

        return lax.ppermute(x, "ctx", [(i, to(i)) for i in range(n_ctx)])

    def swap(x):
        return lax.ppermute(x, "ctx", [(i, i ^ 1) for i in range(n_ctx)])

    q, g = queries[0], out_grad[0]
    packed = jnp.concatenate([keys[0], values[0]], axis=1)
    facing = hop(packed, 1, 0)
    near_in = [hop(packed, 0, dz) for dz in (1, 2, 3)]
    far_in = [hop(facing, 0, 1), hop(near_in[1], 1, 0), hop(facing, 0, 3)]
    mine = [packed] + near_in + [facing] + far_in
    q_par, g_par = swap(q), swap(g)
    others = [swap(x) for x in mine]

    results = run_attention(
        doc_lengths[0].astype(jnp.int32),
        assignment[0].astype(jnp.int32),
        me[None].astype(jnp.int32),
        q,
        q_par,
        g,
        g_par,
        mine + others,
    )
    chips = len(mine)
    own_parts, par_parts = results[:chips], results[chips : chips + n_y]
    dq_own, dq_par = results[chips + n_y :]

    def route(flip):
        pairs = []
        for s in range(n_pipe):
            for i in range(n_ctx):
                to = (s - 1) % n_pipe * n_ctx + (i ^ 1 if flip else i)
                pairs.append((s * n_ctx + i, to))
        return pairs

    def total(parts):
        return functools.reduce(lambda a, b: a + b, [x.astype(jnp.float32) for x in parts])

    far_swap, near_swap = swap(par_parts[1]), swap(par_parts[0])
    dq_same = lax.ppermute(dq_own, ("pipe", "ctx"), route(False))
    dq_flip = lax.ppermute(dq_par, ("pipe", "ctx"), route(True))
    far = [total([own_parts[N_Z + i], far_swap[i]]).astype(jnp.bfloat16) for i in range(N_Z)]
    far2 = hop(far[2], 1, 0)
    far1, far3 = hop(far[1], 0, 1), hop(far[3], 0, 3)
    near = [total([own_parts[i], near_swap[i]]).astype(jnp.bfloat16) for i in (0, 1, 3)]
    near1, near3 = hop(near[1], 0, 1), hop(near[2], 0, 3)
    middle = total([own_parts[2], near_swap[2], far2]).astype(jnp.bfloat16)
    near2 = hop(middle, 0, 2)
    crossed = hop(total([far[0], far1, far3]).astype(jnp.bfloat16), 1, 0)
    kv_grad = total([near[0], near1, near2, near3, crossed])
    kv_out = lax.ppermute(
        kv_grad.astype(jnp.bfloat16), "pipe", [((i + 1) % n_pipe, i) for i in range(n_pipe)]
    )
    left = jnp.where(core == 0, dq_same, dq_flip)
    right = jnp.where(core == 0, dq_flip, dq_same)
    q_out = jnp.concatenate([left, right], axis=1)
    return (q_out[None], kv_out[:, :HD][None], kv_out[:, HD:][None])


def solution(mesh):
    return step_of(mesh, local)


def step_of(mesh, body):
    return jax.shard_map(
        body,
        mesh=mesh,
        in_specs=(
            P("pipe", "ctx", None),
            P("pipe", "ctx", None),
            P("pipe", "ctx", None),
            P("pipe", "ctx", None),
            P("pipe", None),
            P("pipe", None),
        ),
        out_specs=(P("pipe", "ctx", None), P("pipe", "ctx", None), P("pipe", "ctx", None)),
        check_vma=False,
    )
```

```python
import functools
import math

import jax
import jax.numpy as jnp
from jax import lax
from jax.experimental import pallas as pl
from jax.experimental.pallas import tpu as pltpu
from jax.sharding import PartitionSpec as P


BLK = 256
HD = 128
WINDOW = 17
N_Z = 4
CHUNKS = 2
FAR = 262144.0
EXP_SCALE = math.log2(math.e) / math.sqrt(HD)
SCALE = 1.0 / math.sqrt(HD)


def attention_kernel(
    table, *refs, blocks, heads, chips
):
    q_own, q_par, g_own, g_par = refs[:4]
    pieces = refs[4 : 4 + 2 * chips]
    refs = refs[4 + 2 * chips :]
    own_outs, par_outs, dq_own, dq_par = refs[:chips], refs[chips : chips + 2], *refs[chips + 2 : chips + 4]
    (kv, key_mask, kt, dk, dv, q, g, dq, dqt, stage, even, odd, sem, osem) = refs[chips + 4 :]
    nblk = kv.shape[0]
    half = blocks // 2
    items = blocks * heads
    me = table[0]
    docs_at = 1 + 2 * chips
    n_docs = table.shape[0] - docs_at
    core = lax.rem(me, 2)

    def chip_at(sign, r, swap):
        dy, dz = r // N_Z, r % N_Z
        y = lax.rem(me // (2 * N_Z) + dy, chips // N_Z)
        z = lax.rem(lax.rem(me // 2, N_Z) + sign * dz + N_Z, N_Z)
        return table[1 + y * 2 * N_Z + z * 2 + (1 - core if swap else core)]

    copies = []
    for i in range(2 * chips):
        at = chip_at(-1, i % chips, i >= chips)
        copies.append(pltpu.make_async_copy(pieces[i].at[pl.ds(0, BLK)], kv.at[at], sem.at[0]))
        copies.append(
            pltpu.make_async_copy(pieces[i].at[pl.ds(BLK, BLK)], kv.at[nblk - 1 - at], sem.at[0])
        )
    for c in copies:
        c.start()

    own, par = table[1 + me], table[2 + me - 2 * core]
    starts, ends = [], []
    at = jnp.int32(0)
    for i in range(n_docs):
        starts.append(at)
        at = at + table[docs_at + i]
        ends.append(at)

    def first_tile(b):
        reach = jnp.int32(0)
        for x in starts:
            reach = jnp.where(x <= b * BLK, x, reach)
        return reach // BLK

    query_blocks, firsts, halves = [], [], []
    for local, x in enumerate((own, par)):
        y = nblk - 1 - x
        x_low, y_low = first_tile(x), first_tile(y)
        less = (x - x_low) < (y - y_low)
        flip = less == (local == 1)
        query_blocks += [jnp.where(flip, y, x), jnp.where(flip, x, y)]
        firsts += [jnp.where(flip, y_low, x_low), jnp.where(flip, x_low, y_low)]
        second = flip.astype(jnp.int32)
        halves += [second, 1 - second]
    more = []
    for n in range(blocks):
        q_src, g_src = ((q_own, g_own), (q_par, g_par))[n // half]
        at_row = pl.multiple_of(halves[n] * BLK, BLK)
        for h in range(heads):
            col = pl.multiple_of((core * heads + h) * HD, HD)
            for source, target in ((q_src, q), (g_src, g)):
                more.append(
                    pltpu.make_async_copy(
                        source.at[pl.ds(at_row, BLK), pl.ds(col, HD)], target.at[n, h], sem.at[0]
                    )
                )
    for c in more:
        c.start()
    copies += more
    lane = lax.broadcasted_iota(jnp.int32, (BLK, HD), 1)
    row = lax.broadcasted_iota(jnp.int32, (BLK, HD), 0)
    lane_start = jnp.full((BLK, HD), nblk * BLK, jnp.int32)
    lane_end = lane_start
    for i in range(n_docs):
        lane_start = jnp.where(lane == i, starts[i], lane_start)
        lane_end = jnp.where(lane == i, ends[i], lane_end)
    lane_start, lane_end = lane_start - row, lane_end - row

    def inside(b):
        return (lane_start <= b * BLK) & (b * BLK < lane_end)

    def clear(b, carry):
        dk[b] = jnp.zeros(dk.shape[1:], dk.dtype)
        dv[b] = jnp.zeros(dv.shape[1:], dv.dtype)
        key_mask[b] = jnp.where(inside(b), 0.0, 1.0).astype(jnp.bfloat16)
        return carry

    lax.fori_loop(0, nblk, clear, 0)
    for c in copies:
        c.wait()

    def turn(b, carry):
        used = False
        for top, low in zip(query_blocks, firsts):
            used = used | ((b <= top) & (b >= low))

        @pl.when(used)
        def _():
            kt[b] = kv[b, :, :HD].T

        return carry

    lax.fori_loop(0, nblk, turn, 0)

    def choose(n, options):
        out = options[-1]
        for i in range(len(options) - 1):
            out = jnp.where(n == i, options[i], out)
        return out

    def span(i):
        n = i // heads
        b, lo = choose(n, query_blocks), choose(n, firsts)
        return b, lo, b - lo

    def prepare(i, b, bufs):
        qa, gt = bufs[:2]
        n, h = i // heads, lax.rem(i, heads)
        qa[:HD] = q[n, h].T
        qa[HD:] = jnp.where(inside(b), -FAR, 0.0).astype(jnp.bfloat16).T
        gt[...] = g[n, h].T

    def stats(tile, slot, bufs, state, causal, size):
        qa, gt, ebuf, dbuf, mbuf = bufs
        m, l, d = state
        rows = size * BLK
        kvs = kv[pl.ds(tile, size)].reshape(rows, 2 * HD)
        lhs = jnp.concatenate([kvs[:, :HD], key_mask[pl.ds(tile, size)].reshape(rows, HD)], axis=1)
        s = jnp.dot(lhs, qa[...], preferred_element_type=jnp.float32)
        if causal:
            key_at = lax.broadcasted_iota(jnp.int32, s.shape, 0)
            query_at = lax.broadcasted_iota(jnp.int32, s.shape, 1)
            s = jnp.where(key_at <= query_at, s, -FAR)
        dp = jnp.dot(kvs[:, HD:], gt[...], preferred_element_type=jnp.float32)
        step = BLK // 8 // CHUNKS
        s = s.reshape(size * CHUNKS, step, 8, BLK)
        dp = dp.reshape(size * CHUNKS, step, 8, BLK)
        for c in range(size * CHUNKS):
            at, part = slot + c // CHUNKS, pl.ds(c % CHUNKS * step, step)
            sc, dpc = s[c], dp[c]
            top = jnp.maximum(m, jnp.max(sc, axis=0))
            e = jnp.exp2((sc - top[None]) * EXP_SCALE)
            shrink = jnp.exp2((m - top) * EXP_SCALE)
            ebuf[at, part] = e
            dbuf[at, part] = dpc
            mbuf[at, c % CHUNKS] = top
            m, l, d = (
                top,
                l * shrink + jnp.sum(e, axis=0),
                d * shrink + jnp.sum(e * dpc, axis=0),
            )
        return (m, l, d)

    def grads(tile, slot, bufs, n, h, final, size):
        _, _, ebuf, dbuf, mbuf = bufs
        top, inverse, delta = final
        step = BLK // 8 // CHUNKS
        probs, scores = [], []
        for c in range(size * CHUNKS):
            at, part = slot + c // CHUNKS, pl.ds(c % CHUNKS * step, step)
            fix = jnp.exp2((mbuf[at, c % CHUNKS] - top) * EXP_SCALE) * inverse
            p = ebuf[at, part] * fix[None]
            ds = p * (dbuf[at, part] - delta[None])
            probs.append(p.reshape(BLK // CHUNKS, BLK).astype(jnp.bfloat16))
            scores.append(ds.reshape(BLK // CHUNKS, BLK).astype(jnp.bfloat16))
        p = jnp.concatenate(probs, axis=0)
        ds = jnp.concatenate(scores, axis=0)
        keys_t = jnp.concatenate([kt[tile + i] for i in range(size)], axis=1)
        dqt[...] += jnp.dot(keys_t, ds, preferred_element_type=jnp.float32)
        shape = (size, BLK, HD)
        dv[pl.ds(tile, size)] += jnp.dot(
            p, g[n, h], preferred_element_type=jnp.float32
        ).reshape(shape)
        dk[pl.ds(tile, size)] += jnp.dot(
            ds, q[n, h], preferred_element_type=jnp.float32
        ).reshape(shape)

    def finish(state):
        m, l, d = state
        top = jnp.max(m, axis=0, keepdims=True)
        shrink = jnp.exp2((m - top) * EXP_SCALE)
        inverse = 1.0 / jnp.sum(l * shrink, axis=0, keepdims=True)
        delta = jnp.sum(d * shrink, axis=0, keepdims=True) * inverse
        return (top, inverse, delta)

    none = jnp.full((8, BLK), -FAR, jnp.float32)
    zero = jnp.zeros((8, BLK), jnp.float32)
    fresh = (none, zero, zero)

    def sweep(low, high, body, state):
        pairs = (high - low) // 2
        state = lax.fori_loop(0, pairs, lambda t, st: body(low + 2 * t, 2, st), state)
        return lax.fori_loop(low + 2 * pairs, high, lambda t, st: body(t, 1, st), state)

    def start():
        b, lo, count = span(0)
        prepare(0, b, even)
        state = stats(b, count, even, fresh, True, 1)

        def only(t, size, state):
            return stats(lo + t, t, even, state, False, size)

        return finish(sweep(0, count, only, state))

    def step(i, final, now, later):
        n, h = i // heads, lax.rem(i, heads)
        nxt = jnp.minimum(i + 1, items - 1)
        b, lo, count = span(i)
        b_n, lo_n, count_n = span(nxt)
        todo = jnp.where(i + 1 < items, count_n, 0)
        both = jnp.minimum(count, todo) // 2
        prepare(nxt, b_n, later)
        dqt[...] = jnp.zeros_like(dqt)
        state = stats(b_n, count_n, later, fresh, True, 1)
        grads(b, count, now, n, h, final, 1)

        def joint(t, state):
            state = stats(lo_n + 2 * t, 2 * t, later, state, False, 2)
            grads(lo + 2 * t, 2 * t, now, n, h, final, 2)
            return state

        def ahead(t, size, state):
            return stats(lo_n + t, t, later, state, False, size)

        def behind(t, size, carry):
            grads(lo + t, t, now, n, h, final, size)
            return carry

        state = lax.fori_loop(0, both, joint, state)
        state = sweep(2 * both, todo, ahead, state)
        sweep(2 * both, count, behind, 0)
        dq[n, h] = (dqt[...] * SCALE).T.astype(jnp.bfloat16)
        return finish(state)

    def pair(j, final):
        final = step(2 * j, final, even, odd)
        return step(2 * j + 1, final, odd, even)

    lax.fori_loop(0, items // 2, pair, start())

    back = []
    for n in range(blocks):
        at_row = pl.multiple_of(halves[n] * BLK, BLK)
        for h in range(heads):
            back.append(
                pltpu.make_async_copy(
                    dq.at[n, h],
                    (dq_own, dq_par)[n // half].at[pl.ds(at_row, BLK), pl.ds(h * HD, HD)],
                    osem.at[0],
                )
            )
    for c in back:
        c.start()
    for i in list(range(chips + N_Z, 2 * chips)) + list(range(N_Z, chips + N_Z)) + list(range(N_Z)):
        at = chip_at(1, i % chips, i >= chips)
        for first_row, block in ((0, at), (BLK, nblk - 1 - at)):
            stage[i, pl.ds(first_row, BLK), :HD] = (dk[block] * SCALE).astype(jnp.bfloat16)
            stage[i, pl.ds(first_row, BLK), HD:] = dv[block].astype(jnp.bfloat16)
        out = own_outs[i] if i < chips else par_outs[(i - chips) // N_Z].at[i % N_Z]
        c = pltpu.make_async_copy(stage.at[i], out, osem.at[0])
        c.start()
        back.append(c)
    for c in back:
        c.wait()


def run_attention(table, q_own, q_par, g_own, g_par, pieces):
    chips = len(pieces) // 2
    heads = q_own.shape[1] // HD // 2
    rows = q_own.shape[0]
    blocks, nblk = 2 * rows // BLK, 4 * chips
    hbm = pl.BlockSpec(memory_space=pl.ANY)
    smem = pl.BlockSpec(memory_space=pltpu.SMEM)
    bf16, f32 = jnp.bfloat16, jnp.float32
    part = jax.ShapeDtypeStruct((rows, 2 * HD), bf16)
    parts = jax.ShapeDtypeStruct((N_Z, rows, 2 * HD), bf16)
    grad = jax.ShapeDtypeStruct((rows, heads * HD), bf16)
    work = (
        pltpu.VMEM((2 * HD, BLK), bf16),
        pltpu.VMEM((HD, BLK), bf16),
        pltpu.VMEM((WINDOW, BLK // 8, 8, BLK), f32),
        pltpu.VMEM((WINDOW, BLK // 8, 8, BLK), f32),
        pltpu.VMEM((WINDOW, CHUNKS, 8, BLK), f32),
    )
    return pl.pallas_call(
        functools.partial(attention_kernel, blocks=blocks, heads=heads, chips=chips),
        out_shape=[part] * chips + [parts] * (chips // N_Z) + [grad] * 2,
        in_specs=[smem] + [hbm] * (4 + 2 * chips),
        out_specs=[hbm] * (chips + chips // N_Z + 2),
        scratch_shapes=[
            pltpu.VMEM((nblk, BLK, 2 * HD), bf16),
            pltpu.VMEM((nblk, BLK, HD), bf16),
            pltpu.VMEM((nblk, HD, BLK), bf16),
            pltpu.VMEM((nblk, BLK, HD), f32),
            pltpu.VMEM((nblk, BLK, HD), f32),
            pltpu.VMEM((blocks, heads, BLK, HD), bf16),
            pltpu.VMEM((blocks, heads, BLK, HD), bf16),
            pltpu.VMEM((blocks, heads, BLK, HD), bf16),
            pltpu.VMEM((HD, BLK), f32),
            pltpu.VMEM((2 * chips, rows, 2 * HD), bf16),
            work,
            work,
            pltpu.SemaphoreType.DMA((1,)),
            pltpu.SemaphoreType.DMA((1,)),
        ],
        compiler_params=pltpu.CompilerParams(vmem_limit_bytes=46 * 1024 * 1024),
        name="attention",
    )(table, q_own, q_par, g_own, g_par, *pieces)


def local(queries, keys, values, out_grad, doc_lengths, assignment):
    n_ctx = lax.axis_size("ctx")
    n_pipe = lax.axis_size("pipe")
    me = lax.axis_index("ctx")
    core = me % 2
    n_y = n_ctx // 2 // N_Z

    def hop(x, dy, dz):
        def to(i):
            y, z, c = i // (2 * N_Z), i // 2 % N_Z, i % 2
            return ((y + dy) % n_y) * 2 * N_Z + ((z + dz) % N_Z) * 2 + c

        return lax.ppermute(x, "ctx", [(i, to(i)) for i in range(n_ctx)])

    def swap(x):
        return lax.ppermute(x, "ctx", [(i, i ^ 1) for i in range(n_ctx)])

    q, g = queries[0], out_grad[0]
    packed = jnp.concatenate([keys[0], values[0]], axis=1)
    facing = hop(packed, 1, 0)
    near_in = [hop(packed, 0, dz) for dz in (1, 2, 3)]
    far_in = [hop(facing, 0, 1), hop(near_in[1], 1, 0), hop(facing, 0, 3)]
    mine = [packed] + near_in + [facing] + far_in
    q_par, g_par = swap(q), swap(g)
    others = [swap(x) for x in mine]

    results = run_attention(
        jnp.concatenate([me[None], assignment[0], doc_lengths[0]]).astype(jnp.int32),
        q,
        q_par,
        g,
        g_par,
        mine + others,
    )
    chips = len(mine)
    own_parts, par_parts = results[:chips], results[chips : chips + n_y]
    dq_own, dq_par = results[chips + n_y :]

    def route(flip):
        pairs = []
        for s in range(n_pipe):
            for i in range(n_ctx):
                to = (s - 1) % n_pipe * n_ctx + (i ^ 1 if flip else i)
                pairs.append((s * n_ctx + i, to))
        return pairs

    def total(parts):
        return functools.reduce(lambda a, b: a + b, [x.astype(jnp.float32) for x in parts])

    far_swap, near_swap = swap(par_parts[1]), swap(par_parts[0])
    dq_same = lax.ppermute(dq_own, ("pipe", "ctx"), route(False))
    dq_flip = lax.ppermute(dq_par, ("pipe", "ctx"), route(True))
    far = [total([own_parts[N_Z + i], far_swap[i]]).astype(jnp.bfloat16) for i in range(N_Z)]
    far = lax.optimization_barrier(far)
    far2 = hop(far[2], 1, 0)
    far1, far3 = hop(far[1], 0, 1), hop(far[3], 0, 3)
    near = [total([own_parts[i], near_swap[i]]).astype(jnp.bfloat16) for i in (0, 1, 3)]
    near0, near1, near3, near_swap = lax.optimization_barrier((*near, near_swap))
    near1, near3 = hop(near1, 0, 1), hop(near3, 0, 3)
    middle = total([own_parts[2], near_swap[2], far2]).astype(jnp.bfloat16)
    near2 = hop(middle, 0, 2)

    def across(x, dy):
        pairs = []
        for s in range(n_pipe):
            for i in range(n_ctx):
                to = (s - 1) % n_pipe * n_ctx + (i + dy * 2 * N_Z) % n_ctx
                pairs.append((s * n_ctx + i, to))
        return lax.ppermute(x, ("pipe", "ctx"), pairs)

    crossed = across(total([far[0], far1, far3]).astype(jnp.bfloat16), 1)
    straight = across(total([near0, near1, near2, near3]).astype(jnp.bfloat16), 0)
    kv_out = total([crossed, straight]).astype(jnp.bfloat16)
    left = jnp.where(core == 0, dq_same, dq_flip)
    right = jnp.where(core == 0, dq_flip, dq_same)
    q_out = jnp.concatenate([left, right], axis=1)
    return (q_out[None], kv_out[:, :HD][None], kv_out[:, HD:][None])


def solution(mesh):
    return step_of(mesh, local)


def step_of(mesh, body):
    return jax.shard_map(
        body,
        mesh=mesh,
        in_specs=(
            P("pipe", "ctx", None),
            P("pipe", "ctx", None),
            P("pipe", "ctx", None),
            P("pipe", "ctx", None),
            P("pipe", None),
            P("pipe", None),
        ),
        out_specs=(P("pipe", "ctx", None), P("pipe", "ctx", None), P("pipe", "ctx", None)),
        check_vma=False,
    )
```

```python
import functools
import math

import jax
import jax.numpy as jnp
from jax import lax
from jax.experimental import pallas as pl
from jax.experimental.pallas import tpu as pltpu
from jax.sharding import PartitionSpec as P


BLK = 256
HD = 128
WINDOW = 17
N_Z = 4
CHUNKS = 2
FAR = 262144.0
EXP_SCALE = math.log2(math.e) / math.sqrt(HD)
SCALE = 1.0 / math.sqrt(HD)


def attention_kernel(
    table, *refs, blocks, heads, chips
):
    q_own, q_par, g_own, g_par = refs[:4]
    pieces = refs[4 : 4 + 2 * chips]
    refs = refs[4 + 2 * chips :]
    own_outs, par_outs, dq_own, dq_par = refs[:chips], refs[chips : chips + 2], *refs[chips + 2 : chips + 4]
    (kv, key_mask, kt, dk, dv, q, g, dq, dqt, stage, even, odd, sem, osem) = refs[chips + 4 :]
    nblk = kv.shape[0]
    half = blocks // 2
    items = blocks * heads
    me = table[0]
    docs_at = 1 + 2 * chips
    n_docs = table.shape[0] - docs_at
    core = lax.rem(me, 2)

    def chip_at(sign, r, swap):
        dy, dz = r // N_Z, r % N_Z
        y = lax.rem(me // (2 * N_Z) + dy, chips // N_Z)
        z = lax.rem(lax.rem(me // 2, N_Z) + sign * dz + N_Z, N_Z)
        return table[1 + y * 2 * N_Z + z * 2 + (1 - core if swap else core)]

    copies = []
    for i in range(2 * chips):
        at = chip_at(-1, i % chips, i >= chips)
        copies.append(pltpu.make_async_copy(pieces[i].at[pl.ds(0, BLK)], kv.at[at], sem.at[0]))
        copies.append(
            pltpu.make_async_copy(pieces[i].at[pl.ds(BLK, BLK)], kv.at[nblk - 1 - at], sem.at[0])
        )
    for c in copies:
        c.start()

    own, par = table[1 + me], table[2 + me - 2 * core]
    starts, ends = [], []
    at = jnp.int32(0)
    for i in range(n_docs):
        starts.append(at)
        at = at + table[docs_at + i]
        ends.append(at)

    def first_tile(b):
        reach = jnp.int32(0)
        for x in starts:
            reach = jnp.where(x <= b * BLK, x, reach)
        return reach // BLK

    query_blocks, firsts, halves = [], [], []
    for local, x in enumerate((own, par)):
        y = nblk - 1 - x
        x_low, y_low = first_tile(x), first_tile(y)
        less = (x - x_low) < (y - y_low)
        flip = less == (local == 1)
        query_blocks += [jnp.where(flip, y, x), jnp.where(flip, x, y)]
        firsts += [jnp.where(flip, y_low, x_low), jnp.where(flip, x_low, y_low)]
        second = flip.astype(jnp.int32)
        halves += [second, 1 - second]
    more = []
    for n in range(blocks):
        q_src, g_src = ((q_own, g_own), (q_par, g_par))[n // half]
        at_row = pl.multiple_of(halves[n] * BLK, BLK)
        for h in range(heads):
            col = pl.multiple_of((core * heads + h) * HD, HD)
            for source, target in ((q_src, q), (g_src, g)):
                more.append(
                    pltpu.make_async_copy(
                        source.at[pl.ds(at_row, BLK), pl.ds(col, HD)], target.at[n, h], sem.at[0]
                    )
                )
    for c in more:
        c.start()
    copies += more
    lane = lax.broadcasted_iota(jnp.int32, (BLK, HD), 1)
    row = lax.broadcasted_iota(jnp.int32, (BLK, HD), 0)
    lane_start = jnp.full((BLK, HD), nblk * BLK, jnp.int32)
    lane_end = lane_start
    for i in range(n_docs):
        lane_start = jnp.where(lane == i, starts[i], lane_start)
        lane_end = jnp.where(lane == i, ends[i], lane_end)
    lane_start, lane_end = lane_start - row, lane_end - row

    def inside(b):
        return (lane_start <= b * BLK) & (b * BLK < lane_end)

    def clear(b, carry):
        dk[b] = jnp.zeros(dk.shape[1:], dk.dtype)
        dv[b] = jnp.zeros(dv.shape[1:], dv.dtype)
        key_mask[b] = jnp.where(inside(b), 0.0, 1.0).astype(jnp.bfloat16)
        return carry

    lax.fori_loop(0, nblk, clear, 0)
    for c in copies:
        c.wait()

    def turn(b, carry):
        used = False
        for top, low in zip(query_blocks, firsts):
            used = used | ((b <= top) & (b >= low))

        @pl.when(used)
        def _():
            kt[b] = kv[b, :, :HD].T

        return carry

    lax.fori_loop(0, nblk, turn, 0)

    def choose(n, options):
        out = options[-1]
        for i in range(len(options) - 1):
            out = jnp.where(n == i, options[i], out)
        return out

    def span(i):
        n = i // heads
        b, lo = choose(n, query_blocks), choose(n, firsts)
        return b, lo, b - lo

    def prepare(i, b, bufs):
        qa, gt = bufs[:2]
        n, h = i // heads, lax.rem(i, heads)
        qa[:HD] = q[n, h].T
        qa[HD:] = jnp.where(inside(b), -FAR, 0.0).astype(jnp.bfloat16).T
        gt[...] = g[n, h].T

    def stats(tile, slot, bufs, state, causal, size):
        qa, gt, ebuf, dbuf, mbuf = bufs
        m, l, d = state
        rows = size * BLK
        kvs = kv[pl.ds(tile, size)].reshape(rows, 2 * HD)
        lhs = jnp.concatenate([kvs[:, :HD], key_mask[pl.ds(tile, size)].reshape(rows, HD)], axis=1)
        s = jnp.dot(lhs, qa[...], preferred_element_type=jnp.float32)
        if causal:
            key_at = lax.broadcasted_iota(jnp.int32, s.shape, 0)
            query_at = lax.broadcasted_iota(jnp.int32, s.shape, 1)
            s = jnp.where(key_at <= query_at, s, -FAR)
        dp = jnp.dot(kvs[:, HD:], gt[...], preferred_element_type=jnp.float32)
        step = BLK // 8 // CHUNKS
        s = s.reshape(size * CHUNKS, step, 8, BLK)
        dp = dp.reshape(size * CHUNKS, step, 8, BLK)
        for c in range(size * CHUNKS):
            at, part = slot + c // CHUNKS, pl.ds(c % CHUNKS * step, step)
            sc, dpc = s[c], dp[c]
            top = jnp.maximum(m, jnp.max(sc, axis=0))
            e = jnp.exp2((sc - top[None]) * EXP_SCALE)
            shrink = jnp.exp2((m - top) * EXP_SCALE)
            ebuf[at, part] = e
            dbuf[at, part] = dpc
            mbuf[at, c % CHUNKS] = top
            m, l, d = (
                top,
                l * shrink + jnp.sum(e, axis=0),
                d * shrink + jnp.sum(e * dpc, axis=0),
            )
        return (m, l, d)

    def grads(tile, slot, bufs, n, h, final, size):
        _, _, ebuf, dbuf, mbuf = bufs
        top, inverse, delta = final
        step = BLK // 8 // CHUNKS
        probs, scores = [], []
        for c in range(size * CHUNKS):
            at, part = slot + c // CHUNKS, pl.ds(c % CHUNKS * step, step)
            fix = jnp.exp2((mbuf[at, c % CHUNKS] - top) * EXP_SCALE) * inverse
            p = ebuf[at, part] * fix[None]
            ds = p * (dbuf[at, part] - delta[None])
            probs.append(p.reshape(BLK // CHUNKS, BLK).astype(jnp.bfloat16))
            scores.append(ds.reshape(BLK // CHUNKS, BLK).astype(jnp.bfloat16))
        p = jnp.concatenate(probs, axis=0)
        ds = jnp.concatenate(scores, axis=0)
        keys_t = jnp.concatenate([kt[tile + i] for i in range(size)], axis=1)
        dqt[...] += jnp.dot(keys_t, ds, preferred_element_type=jnp.float32)
        shape = (size, BLK, HD)
        dv[pl.ds(tile, size)] += jnp.dot(
            p, g[n, h], preferred_element_type=jnp.float32
        ).reshape(shape)
        dk[pl.ds(tile, size)] += jnp.dot(
            ds, q[n, h], preferred_element_type=jnp.float32
        ).reshape(shape)

    def finish(state):
        m, l, d = state
        top = jnp.max(m, axis=0, keepdims=True)
        shrink = jnp.exp2((m - top) * EXP_SCALE)
        inverse = 1.0 / jnp.sum(l * shrink, axis=0, keepdims=True)
        delta = jnp.sum(d * shrink, axis=0, keepdims=True) * inverse
        return (top, inverse, delta)

    none = jnp.full((8, BLK), -FAR, jnp.float32)
    zero = jnp.zeros((8, BLK), jnp.float32)
    fresh = (none, zero, zero)

    def sweep(low, high, body, state):
        pairs = (high - low) // 2
        state = lax.fori_loop(0, pairs, lambda t, st: body(low + 2 * t, 2, st), state)
        return lax.fori_loop(low + 2 * pairs, high, lambda t, st: body(t, 1, st), state)

    def start():
        b, lo, count = span(0)
        prepare(0, b, even)
        state = stats(b, count, even, fresh, True, 1)

        def only(t, size, state):
            return stats(lo + t, t, even, state, False, size)

        return finish(sweep(0, count, only, state))

    def step(i, final, now, later):
        n, h = i // heads, lax.rem(i, heads)
        nxt = jnp.minimum(i + 1, items - 1)
        b, lo, count = span(i)
        b_n, lo_n, count_n = span(nxt)
        todo = jnp.where(i + 1 < items, count_n, 0)
        both = jnp.minimum(count, todo) // 2
        prepare(nxt, b_n, later)
        dqt[...] = jnp.zeros_like(dqt)
        state = stats(b_n, count_n, later, fresh, True, 1)
        grads(b, count, now, n, h, final, 1)

        def joint(t, state):
            state = stats(lo_n + 2 * t, 2 * t, later, state, False, 2)
            grads(lo + 2 * t, 2 * t, now, n, h, final, 2)
            return state

        def ahead(t, size, state):
            return stats(lo_n + t, t, later, state, False, size)

        def behind(t, size, carry):
            grads(lo + t, t, now, n, h, final, size)
            return carry

        state = lax.fori_loop(0, both, joint, state)
        state = sweep(2 * both, todo, ahead, state)
        sweep(2 * both, count, behind, 0)
        dq[n, h] = (dqt[...] * SCALE).T.astype(jnp.bfloat16)
        return finish(state)

    def pair(j, final):
        final = step(2 * j, final, even, odd)
        return step(2 * j + 1, final, odd, even)

    lax.fori_loop(0, items // 2, pair, start())

    back = []
    for n in range(blocks):
        at_row = pl.multiple_of(halves[n] * BLK, BLK)
        for h in range(heads):
            back.append(
                pltpu.make_async_copy(
                    dq.at[n, h],
                    (dq_own, dq_par)[n // half].at[pl.ds(at_row, BLK), pl.ds(h * HD, HD)],
                    osem.at[0],
                )
            )
    for c in back:
        c.start()
    for i in list(range(chips + N_Z, 2 * chips)) + list(range(N_Z, chips + N_Z)) + list(range(N_Z)):
        at = chip_at(1, i % chips, i >= chips)
        for first_row, block in ((0, at), (BLK, nblk - 1 - at)):
            stage[i, pl.ds(first_row, BLK), :HD] = (dk[block] * SCALE).astype(jnp.bfloat16)
            stage[i, pl.ds(first_row, BLK), HD:] = dv[block].astype(jnp.bfloat16)
        out = own_outs[i] if i < chips else par_outs[(i - chips) // N_Z].at[i % N_Z]
        c = pltpu.make_async_copy(stage.at[i], out, osem.at[0])
        c.start()
        back.append(c)
    for c in back:
        c.wait()


def run_attention(table, q_own, q_par, g_own, g_par, pieces):
    chips = len(pieces) // 2
    heads = q_own.shape[1] // HD // 2
    rows = q_own.shape[0]
    blocks, nblk = 2 * rows // BLK, 4 * chips
    hbm = pl.BlockSpec(memory_space=pl.ANY)
    smem = pl.BlockSpec(memory_space=pltpu.SMEM)
    bf16, f32 = jnp.bfloat16, jnp.float32
    part = jax.ShapeDtypeStruct((rows, 2 * HD), bf16)
    parts = jax.ShapeDtypeStruct((N_Z, rows, 2 * HD), bf16)
    grad = jax.ShapeDtypeStruct((rows, heads * HD), bf16)
    work = (
        pltpu.VMEM((2 * HD, BLK), bf16),
        pltpu.VMEM((HD, BLK), bf16),
        pltpu.VMEM((WINDOW, BLK // 8, 8, BLK), f32),
        pltpu.VMEM((WINDOW, BLK // 8, 8, BLK), f32),
        pltpu.VMEM((WINDOW, CHUNKS, 8, BLK), f32),
    )
    return pl.pallas_call(
        functools.partial(attention_kernel, blocks=blocks, heads=heads, chips=chips),
        out_shape=[part] * chips + [parts] * (chips // N_Z) + [grad] * 2,
        in_specs=[smem] + [hbm] * (4 + 2 * chips),
        out_specs=[hbm] * (chips + chips // N_Z + 2),
        scratch_shapes=[
            pltpu.VMEM((nblk, BLK, 2 * HD), bf16),
            pltpu.VMEM((nblk, BLK, HD), bf16),
            pltpu.VMEM((nblk, HD, BLK), bf16),
            pltpu.VMEM((nblk, BLK, HD), f32),
            pltpu.VMEM((nblk, BLK, HD), f32),
            pltpu.VMEM((blocks, heads, BLK, HD), bf16),
            pltpu.VMEM((blocks, heads, BLK, HD), bf16),
            pltpu.VMEM((blocks, heads, BLK, HD), bf16),
            pltpu.VMEM((HD, BLK), f32),
            pltpu.VMEM((2 * chips, rows, 2 * HD), bf16),
            work,
            work,
            pltpu.SemaphoreType.DMA((1,)),
            pltpu.SemaphoreType.DMA((1,)),
        ],
        compiler_params=pltpu.CompilerParams(vmem_limit_bytes=46 * 1024 * 1024,
       ),
        name="attention",
    )(table, q_own, q_par, g_own, g_par, *pieces)


def local(queries, keys, values, out_grad, doc_lengths, assignment):
    n_ctx = lax.axis_size("ctx")
    n_pipe = lax.axis_size("pipe")
    me = lax.axis_index("ctx")
    core = me % 2
    n_y = n_ctx // 2 // N_Z

    def hop(x, dy, dz):
        def to(i):
            y, z, c = i // (2 * N_Z), i // 2 % N_Z, i % 2
            return ((y + dy) % n_y) * 2 * N_Z + ((z + dz) % N_Z) * 2 + c

        return lax.ppermute(x, "ctx", [(i, to(i)) for i in range(n_ctx)])

    def swap(x):
        return lax.ppermute(x, "ctx", [(i, i ^ 1) for i in range(n_ctx)])

    q, g = queries[0], out_grad[0]
    packed = jnp.concatenate([keys[0], values[0]], axis=1)
    facing = hop(packed, 1, 0)
    near_in = [hop(packed, 0, dz) for dz in (1, 2, 3)]
    far_in = [hop(facing, 0, 1), hop(near_in[1], 1, 0), hop(facing, 0, 3)]
    mine = [packed] + near_in + [facing] + far_in
    q_par, g_par = swap(q), swap(g)
    others = [swap(x) for x in mine]

    results = run_attention(
        jnp.concatenate([me[None], assignment[0], doc_lengths[0]]).astype(jnp.int32),
        q,
        q_par,
        g,
        g_par,
        mine + others,
    )
    chips = len(mine)
    own_parts, par_parts = results[:chips], results[chips : chips + n_y]
    dq_own, dq_par = results[chips + n_y :]

    def route(flip):
        pairs = []
        for s in range(n_pipe):
            for i in range(n_ctx):
                to = (s - 1) % n_pipe * n_ctx + (i ^ 1 if flip else i)
                pairs.append((s * n_ctx + i, to))
        return pairs

    def total(parts):
        return functools.reduce(lambda a, b: a + b, [x.astype(jnp.float32) for x in parts])

    far_swap, near_swap = swap(par_parts[1]), swap(par_parts[0])
    dq_same = lax.ppermute(dq_own, ("pipe", "ctx"), route(False))
    dq_flip = lax.ppermute(dq_par, ("pipe", "ctx"), route(True))
    far = [total([own_parts[N_Z + i], far_swap[i]]).astype(jnp.bfloat16) for i in range(N_Z)]
    far = lax.optimization_barrier(far)
    far_in = [hop(far[dz], 0, dz) for dz in (1, 2, 3)]
    near = [total([own_parts[i], near_swap[i]]).astype(jnp.bfloat16) for i in range(N_Z)]
    near_in = [hop(near[dz], 0, dz) for dz in (1, 2, 3)]

    def across(x, dy):
        pairs = []
        for s in range(n_pipe):
            for i in range(n_ctx):
                to = (s - 1) % n_pipe * n_ctx + (i + dy * 2 * N_Z) % n_ctx
                pairs.append((s * n_ctx + i, to))
        return lax.ppermute(x, ("pipe", "ctx"), pairs)

    crossed = across(total([far[0]] + far_in).astype(jnp.bfloat16), 1)
    straight = across(total([near[0]] + near_in).astype(jnp.bfloat16), 0)
    kv_out = total([crossed, straight]).astype(jnp.bfloat16)
    left = jnp.where(core == 0, dq_same, dq_flip)
    right = jnp.where(core == 0, dq_flip, dq_same)
    q_out = jnp.concatenate([left, right], axis=1)
    return (q_out[None], kv_out[:, :HD][None], kv_out[:, HD:][None])


def solution(mesh):
    return step_of(mesh, local)


def step_of(mesh, body):
    return jax.shard_map(
        body,
        mesh=mesh,
        in_specs=(
            P("pipe", "ctx", None),
            P("pipe", "ctx", None),
            P("pipe", "ctx", None),
            P("pipe", "ctx", None),
            P("pipe", None),
            P("pipe", None),
        ),
        out_specs=(P("pipe", "ctx", None), P("pipe", "ctx", None), P("pipe", "ctx", None)),
        check_vma=False,
    )
```

```python
import functools
import math

import jax
import jax.numpy as jnp
from jax import lax
from jax.experimental import pallas as pl
from jax.experimental.pallas import tpu as pltpu
from jax.sharding import PartitionSpec as P


BLK = 256
HD = 128
WINDOW = 17
N_Z = 4
CHUNKS = 2
FAR = 262144.0
EXP_SCALE = math.log2(math.e) / math.sqrt(HD)
SCALE = 1.0 / math.sqrt(HD)


def attention_kernel(
    table, *refs, blocks, heads, chips
):
    q_own, q_par, g_own, g_par = refs[:4]
    pieces = refs[4 : 4 + 2 * chips]
    refs = refs[4 + 2 * chips :]
    own_outs, par_outs, dq_own, dq_par = refs[:chips], refs[chips : chips + 2], *refs[chips + 2 : chips + 4]
    (kv, key_mask, kt, dk, dv, q, g, dq, dqt, stage, even, odd, sem, osem) = refs[chips + 4 :]
    nblk = kv.shape[0]
    half = blocks // 2
    items = blocks * heads
    me = table[0]
    docs_at = 1 + 2 * chips
    n_docs = table.shape[0] - docs_at
    core = lax.rem(me, 2)

    def chip_at(sign, r, swap):
        dy, dz = r // N_Z, r % N_Z
        y = lax.rem(me // (2 * N_Z) + dy, chips // N_Z)
        z = lax.rem(lax.rem(me // 2, N_Z) + sign * dz + N_Z, N_Z)
        return table[1 + y * 2 * N_Z + z * 2 + (1 - core if swap else core)]

    copies = []
    for i in range(2 * chips):
        at = chip_at(-1, i % chips, i >= chips)
        copies.append(pltpu.make_async_copy(pieces[i].at[pl.ds(0, BLK)], kv.at[at], sem.at[0]))
        copies.append(
            pltpu.make_async_copy(pieces[i].at[pl.ds(BLK, BLK)], kv.at[nblk - 1 - at], sem.at[0])
        )
    for c in copies:
        c.start()

    own, par = table[1 + me], table[2 + me - 2 * core]
    starts, ends = [], []
    at = jnp.int32(0)
    for i in range(n_docs):
        starts.append(at)
        at = at + table[docs_at + i]
        ends.append(at)

    def first_tile(b):
        reach = jnp.int32(0)
        for x in starts:
            reach = jnp.where(x <= b * BLK, x, reach)
        return reach // BLK

    query_blocks, firsts, halves = [], [], []
    for local, x in enumerate((own, par)):
        y = nblk - 1 - x
        x_low, y_low = first_tile(x), first_tile(y)
        less = (x - x_low) < (y - y_low)
        flip = less == (local == 1)
        query_blocks += [jnp.where(flip, y, x), jnp.where(flip, x, y)]
        firsts += [jnp.where(flip, y_low, x_low), jnp.where(flip, x_low, y_low)]
        second = flip.astype(jnp.int32)
        halves += [second, 1 - second]
    more = []
    for n in range(blocks):
        q_src, g_src = ((q_own, g_own), (q_par, g_par))[n // half]
        at_row = pl.multiple_of(halves[n] * BLK, BLK)
        for h in range(heads):
            col = pl.multiple_of((core * heads + h) * HD, HD)
            for source, target in ((q_src, q), (g_src, g)):
                more.append(
                    pltpu.make_async_copy(
                        source.at[pl.ds(at_row, BLK), pl.ds(col, HD)], target.at[n, h], sem.at[0]
                    )
                )
    for c in more:
        c.start()
    copies += more
    lane = lax.broadcasted_iota(jnp.int32, (BLK, HD), 1)
    row = lax.broadcasted_iota(jnp.int32, (BLK, HD), 0)
    lane_start = jnp.full((BLK, HD), nblk * BLK, jnp.int32)
    lane_end = lane_start
    for i in range(n_docs):
        lane_start = jnp.where(lane == i, starts[i], lane_start)
        lane_end = jnp.where(lane == i, ends[i], lane_end)
    lane_start, lane_end = lane_start - row, lane_end - row

    def inside(b):
        return (lane_start <= b * BLK) & (b * BLK < lane_end)

    def clear(b, carry):
        dk[b] = jnp.zeros(dk.shape[1:], dk.dtype)
        dv[b] = jnp.zeros(dv.shape[1:], dv.dtype)
        key_mask[b] = jnp.where(inside(b), 0.0, 1.0).astype(jnp.bfloat16)
        return carry

    lax.fori_loop(0, nblk, clear, 0)
    for c in copies:
        c.wait()

    def turn(b, carry):
        used = False
        for top, low in zip(query_blocks, firsts):
            used = used | ((b <= top) & (b >= low))

        @pl.when(used)
        def _():
            kt[b] = kv[b, :, :HD].T

        return carry

    lax.fori_loop(0, nblk, turn, 0)

    def choose(n, options):
        out = options[-1]
        for i in range(len(options) - 1):
            out = jnp.where(n == i, options[i], out)
        return out

    def span(i):
        n = i // heads
        b, lo = choose(n, query_blocks), choose(n, firsts)
        return b, lo, b - lo

    def prepare(i, b, bufs):
        qa, gt = bufs[:2]
        n, h = i // heads, lax.rem(i, heads)
        qa[:HD] = q[n, h].T
        qa[HD:] = jnp.where(inside(b), -FAR, 0.0).astype(jnp.bfloat16).T
        gt[...] = g[n, h].T

    def stats(tile, slot, bufs, state, causal, size):
        qa, gt, ebuf, dbuf, mbuf = bufs
        m, l, d = state
        rows = size * BLK
        kvs = kv[pl.ds(tile, size)].reshape(rows, 2 * HD)
        lhs = jnp.concatenate([kvs[:, :HD], key_mask[pl.ds(tile, size)].reshape(rows, HD)], axis=1)
        s = jnp.dot(lhs, qa[...], preferred_element_type=jnp.float32)
        if causal:
            key_at = lax.broadcasted_iota(jnp.int32, s.shape, 0)
            query_at = lax.broadcasted_iota(jnp.int32, s.shape, 1)
            s = jnp.where(key_at <= query_at, s, -FAR)
        dp = jnp.dot(kvs[:, HD:], gt[...], preferred_element_type=jnp.float32)
        step = BLK // 8 // CHUNKS
        s = s.reshape(size * CHUNKS, step, 8, BLK)
        dp = dp.reshape(size * CHUNKS, step, 8, BLK)
        for c in range(size * CHUNKS):
            at, part = slot + c // CHUNKS, pl.ds(c % CHUNKS * step, step)
            sc, dpc = s[c], dp[c]
            top = jnp.maximum(m, jnp.max(sc, axis=0))
            e = jnp.exp2((sc - top[None]) * EXP_SCALE)
            shrink = jnp.exp2((m - top) * EXP_SCALE)
            ebuf[at, part] = e
            dbuf[at, part] = dpc
            mbuf[at, c % CHUNKS] = top
            m, l, d = (
                top,
                l * shrink + jnp.sum(e, axis=0),
                d * shrink + jnp.sum(e * dpc, axis=0),
            )
        return (m, l, d)

    def grads(tile, slot, bufs, n, h, final, size):
        _, _, ebuf, dbuf, mbuf = bufs
        top, inverse, delta = final
        step = BLK // 8 // CHUNKS
        probs, scores = [], []
        for c in range(size * CHUNKS):
            at, part = slot + c // CHUNKS, pl.ds(c % CHUNKS * step, step)
            fix = jnp.exp2((mbuf[at, c % CHUNKS] - top) * EXP_SCALE) * inverse
            p = ebuf[at, part] * fix[None]
            ds = p * (dbuf[at, part] - delta[None])
            probs.append(p.reshape(BLK // CHUNKS, BLK).astype(jnp.bfloat16))
            scores.append(ds.reshape(BLK // CHUNKS, BLK).astype(jnp.bfloat16))
        p = jnp.concatenate(probs, axis=0)
        ds = jnp.concatenate(scores, axis=0)
        keys_t = jnp.concatenate([kt[tile + i] for i in range(size)], axis=1)
        dqt[...] += jnp.dot(keys_t, ds, preferred_element_type=jnp.float32)
        shape = (size, BLK, HD)
        dv[pl.ds(tile, size)] += jnp.dot(
            p, g[n, h], preferred_element_type=jnp.float32
        ).reshape(shape)
        dk[pl.ds(tile, size)] += jnp.dot(
            ds, q[n, h], preferred_element_type=jnp.float32
        ).reshape(shape)

    def finish(state):
        m, l, d = state
        top = jnp.max(m, axis=0, keepdims=True)
        shrink = jnp.exp2((m - top) * EXP_SCALE)
        inverse = 1.0 / jnp.sum(l * shrink, axis=0, keepdims=True)
        delta = jnp.sum(d * shrink, axis=0, keepdims=True) * inverse
        return (top, inverse, delta)

    none = jnp.full((8, BLK), -FAR, jnp.float32)
    zero = jnp.zeros((8, BLK), jnp.float32)
    fresh = (none, zero, zero)

    def sweep(low, high, body, state, size=2):
        full = (high - low) // size
        state = lax.fori_loop(0, full, lambda t, st: body(low + size * t, size, st), state)
        return lax.fori_loop(low + size * full, high, lambda t, st: body(t, 1, st), state)

    def start():
        b, lo, count = span(0)
        prepare(0, b, even)
        state = stats(b, count, even, fresh, True, 1)

        def only(t, size, state):
            return stats(lo + t, t, even, state, False, size)

        return finish(sweep(0, count, only, state))

    def step(i, final, now, later):
        n, h = i // heads, lax.rem(i, heads)
        nxt = jnp.minimum(i + 1, items - 1)
        b, lo, count = span(i)
        b_n, lo_n, count_n = span(nxt)
        todo = jnp.where(i + 1 < items, count_n, 0)
        both = jnp.minimum(count, todo)
        prepare(nxt, b_n, later)
        dqt[...] = jnp.zeros_like(dqt)
        state = stats(b_n, count_n, later, fresh, True, 1)
        grads(b, count, now, n, h, final, 1)

        def joint(t, size, state):
            state = stats(lo_n + t, t, later, state, False, size)
            grads(lo + t, t, now, n, h, final, size)
            return state

        def ahead(t, size, state):
            return stats(lo_n + t, t, later, state, False, size)

        def behind(t, size, carry):
            grads(lo + t, t, now, n, h, final, size)
            return carry

        state = sweep(0, both, joint, state, 3)
        state = sweep(both, todo, ahead, state)
        sweep(both, count, behind, 0)
        dq[n, h] = (dqt[...] * SCALE).T.astype(jnp.bfloat16)
        return finish(state)

    def pair(j, final):
        final = step(2 * j, final, even, odd)
        return step(2 * j + 1, final, odd, even)

    lax.fori_loop(0, items // 2, pair, start())

    back = []
    for n in range(blocks):
        at_row = pl.multiple_of(halves[n] * BLK, BLK)
        for h in range(heads):
            back.append(
                pltpu.make_async_copy(
                    dq.at[n, h],
                    (dq_own, dq_par)[n // half].at[pl.ds(at_row, BLK), pl.ds(h * HD, HD)],
                    osem.at[0],
                )
            )
    for c in back:
        c.start()
    for i in list(range(chips + N_Z, 2 * chips)) + list(range(N_Z, chips + N_Z)) + list(range(N_Z)):
        at = chip_at(1, i % chips, i >= chips)
        for first_row, block in ((0, at), (BLK, nblk - 1 - at)):
            stage[i, pl.ds(first_row, BLK), :HD] = (dk[block] * SCALE).astype(jnp.bfloat16)
            stage[i, pl.ds(first_row, BLK), HD:] = dv[block].astype(jnp.bfloat16)
        out = own_outs[i] if i < chips else par_outs[(i - chips) // N_Z].at[i % N_Z]
        c = pltpu.make_async_copy(stage.at[i], out, osem.at[0])
        c.start()
        back.append(c)
    for c in back:
        c.wait()


def run_attention(table, q_own, q_par, g_own, g_par, pieces):
    chips = len(pieces) // 2
    heads = q_own.shape[1] // HD // 2
    rows = q_own.shape[0]
    blocks, nblk = 2 * rows // BLK, 4 * chips
    hbm = pl.BlockSpec(memory_space=pl.ANY)
    smem = pl.BlockSpec(memory_space=pltpu.SMEM)
    bf16, f32 = jnp.bfloat16, jnp.float32
    part = jax.ShapeDtypeStruct((rows, 2 * HD), bf16)
    parts = jax.ShapeDtypeStruct((N_Z, rows, 2 * HD), bf16)
    grad = jax.ShapeDtypeStruct((rows, heads * HD), bf16)
    work = (
        pltpu.VMEM((2 * HD, BLK), bf16),
        pltpu.VMEM((HD, BLK), bf16),
        pltpu.VMEM((WINDOW, BLK // 8, 8, BLK), f32),
        pltpu.VMEM((WINDOW, BLK // 8, 8, BLK), f32),
        pltpu.VMEM((WINDOW, CHUNKS, 8, BLK), f32),
    )
    return pl.pallas_call(
        functools.partial(attention_kernel, blocks=blocks, heads=heads, chips=chips),
        out_shape=[part] * chips + [parts] * (chips // N_Z) + [grad] * 2,
        in_specs=[smem] + [hbm] * (4 + 2 * chips),
        out_specs=[hbm] * (chips + chips // N_Z + 2),
        scratch_shapes=[
            pltpu.VMEM((nblk, BLK, 2 * HD), bf16),
            pltpu.VMEM((nblk, BLK, HD), bf16),
            pltpu.VMEM((nblk, HD, BLK), bf16),
            pltpu.VMEM((nblk, BLK, HD), f32),
            pltpu.VMEM((nblk, BLK, HD), f32),
            pltpu.VMEM((blocks, heads, BLK, HD), bf16),
            pltpu.VMEM((blocks, heads, BLK, HD), bf16),
            pltpu.VMEM((blocks, heads, BLK, HD), bf16),
            pltpu.VMEM((HD, BLK), f32),
            pltpu.VMEM((2 * chips, rows, 2 * HD), bf16),
            work,
            work,
            pltpu.SemaphoreType.DMA((1,)),
            pltpu.SemaphoreType.DMA((1,)),
        ],
        compiler_params=pltpu.CompilerParams(vmem_limit_bytes=46 * 1024 * 1024,
       ),
        name="attention",
    )(table, q_own, q_par, g_own, g_par, *pieces)


def local(queries, keys, values, out_grad, doc_lengths, assignment):
    n_ctx = lax.axis_size("ctx")
    n_pipe = lax.axis_size("pipe")
    me = lax.axis_index("ctx")
    core = me % 2
    n_y = n_ctx // 2 // N_Z

    def hop(x, dy, dz):
        def to(i):
            y, z, c = i // (2 * N_Z), i // 2 % N_Z, i % 2
            return ((y + dy) % n_y) * 2 * N_Z + ((z + dz) % N_Z) * 2 + c

        return lax.ppermute(x, "ctx", [(i, to(i)) for i in range(n_ctx)])

    def swap(x):
        return lax.ppermute(x, "ctx", [(i, i ^ 1) for i in range(n_ctx)])

    q, g = queries[0], out_grad[0]
    packed = jnp.concatenate([keys[0], values[0]], axis=1)
    facing = hop(packed, 1, 0)
    near_in = [hop(packed, 0, dz) for dz in (1, 2, 3)]
    far_in = [hop(facing, 0, 1), hop(near_in[1], 1, 0), hop(facing, 0, 3)]
    mine = [packed] + near_in + [facing] + far_in
    q_par, g_par = swap(q), swap(g)
    others = [swap(x) for x in mine]

    results = run_attention(
        jnp.concatenate([me[None], assignment[0], doc_lengths[0]]).astype(jnp.int32),
        q,
        q_par,
        g,
        g_par,
        mine + others,
    )
    chips = len(mine)
    own_parts, par_parts = results[:chips], results[chips : chips + n_y]
    dq_own, dq_par = results[chips + n_y :]

    def route(flip):
        pairs = []
        for s in range(n_pipe):
            for i in range(n_ctx):
                to = (s - 1) % n_pipe * n_ctx + (i ^ 1 if flip else i)
                pairs.append((s * n_ctx + i, to))
        return pairs

    def total(parts):
        return functools.reduce(lambda a, b: a + b, [x.astype(jnp.float32) for x in parts])

    far_swap, near_swap = swap(par_parts[1]), swap(par_parts[0])
    dq_same = lax.ppermute(dq_own, ("pipe", "ctx"), route(False))
    dq_flip = lax.ppermute(dq_par, ("pipe", "ctx"), route(True))
    far = [total([own_parts[N_Z + i], far_swap[i]]).astype(jnp.bfloat16) for i in range(N_Z)]
    far = lax.optimization_barrier(far)
    far_in = [hop(far[dz], 0, dz) for dz in (1, 2, 3)]
    near = [total([own_parts[i], near_swap[i]]).astype(jnp.bfloat16) for i in range(N_Z)]
    near_in = [hop(near[dz], 0, dz) for dz in (1, 2, 3)]

    def across(x, dy):
        pairs = []
        for s in range(n_pipe):
            for i in range(n_ctx):
                to = (s - 1) % n_pipe * n_ctx + (i + dy * 2 * N_Z) % n_ctx
                pairs.append((s * n_ctx + i, to))
        return lax.ppermute(x, ("pipe", "ctx"), pairs)

    crossed = across(total([far[0]] + far_in).astype(jnp.bfloat16), 1)
    straight = across(total([near[0]] + near_in).astype(jnp.bfloat16), 0)
    kv_out = total([crossed, straight]).astype(jnp.bfloat16)
    left = jnp.where(core == 0, dq_same, dq_flip)
    right = jnp.where(core == 0, dq_flip, dq_same)
    q_out = jnp.concatenate([left, right], axis=1)
    return (q_out[None], kv_out[:, :HD][None], kv_out[:, HD:][None])


def solution(mesh):
    return step_of(mesh, local)


def step_of(mesh, body):
    return jax.shard_map(
        body,
        mesh=mesh,
        in_specs=(
            P("pipe", "ctx", None),
            P("pipe", "ctx", None),
            P("pipe", "ctx", None),
            P("pipe", "ctx", None),
            P("pipe", None),
            P("pipe", None),
        ),
        out_specs=(P("pipe", "ctx", None), P("pipe", "ctx", None), P("pipe", "ctx", None)),
        check_vma=False,
    )
```

```python
import functools
import math

import jax
import jax.numpy as jnp
from jax import lax
from jax.experimental import pallas as pl
from jax.experimental.pallas import tpu as pltpu
from jax.sharding import PartitionSpec as P


BLK = 256
HD = 128
WINDOW = 17
N_Z = 4
CHUNKS = 2
FAR = 262144.0
EXP_SCALE = math.log2(math.e) / math.sqrt(HD)
SCALE = 1.0 / math.sqrt(HD)


def attention_kernel(
    table, *refs, blocks, heads, chips
):
    q_own, q_par, g_own, g_par = refs[:4]
    pieces = refs[4 : 4 + 2 * chips]
    refs = refs[4 + 2 * chips :]
    own_outs, par_outs, dq_own, dq_par = refs[:chips], refs[chips : chips + 2], *refs[chips + 2 : chips + 4]
    (kv, key_mask, kt, dk, dv, q, g, dq, dqt, stage, even, odd, sem, osem) = refs[chips + 4 :]
    nblk = kv.shape[0]
    half = blocks // 2
    items = blocks * heads
    me = table[0]
    docs_at = 1 + 2 * chips
    n_docs = table.shape[0] - docs_at
    core = lax.rem(me, 2)

    def chip_at(sign, r, swap):
        dy, dz = r // N_Z, r % N_Z
        y = lax.rem(me // (2 * N_Z) + dy, chips // N_Z)
        z = lax.rem(lax.rem(me // 2, N_Z) + sign * dz + N_Z, N_Z)
        return table[1 + y * 2 * N_Z + z * 2 + (1 - core if swap else core)]

    copies = []
    for i in range(2 * chips):
        at = chip_at(-1, i % chips, i >= chips)
        copies.append(pltpu.make_async_copy(pieces[i].at[pl.ds(0, BLK)], kv.at[at], sem.at[0]))
        copies.append(
            pltpu.make_async_copy(pieces[i].at[pl.ds(BLK, BLK)], kv.at[nblk - 1 - at], sem.at[0])
        )
    for c in copies:
        c.start()

    own, par = table[1 + me], table[2 + me - 2 * core]
    starts, ends = [], []
    at = jnp.int32(0)
    for i in range(n_docs):
        starts.append(at)
        at = at + table[docs_at + i]
        ends.append(at)

    def first_tile(b):
        reach = jnp.int32(0)
        for x in starts:
            reach = jnp.where(x <= b * BLK, x, reach)
        return reach // BLK

    query_blocks, firsts, halves = [], [], []
    for local, x in enumerate((own, par)):
        y = nblk - 1 - x
        x_low, y_low = first_tile(x), first_tile(y)
        less = (x - x_low) < (y - y_low)
        flip = less == (local == 1)
        query_blocks += [jnp.where(flip, y, x), jnp.where(flip, x, y)]
        firsts += [jnp.where(flip, y_low, x_low), jnp.where(flip, x_low, y_low)]
        second = flip.astype(jnp.int32)
        halves += [second, 1 - second]
    more = []
    for n in range(blocks):
        q_src, g_src = ((q_own, g_own), (q_par, g_par))[n // half]
        at_row = pl.multiple_of(halves[n] * BLK, BLK)
        for h in range(heads):
            col = pl.multiple_of((core * heads + h) * HD, HD)
            for source, target in ((q_src, q), (g_src, g)):
                more.append(
                    pltpu.make_async_copy(
                        source.at[pl.ds(at_row, BLK), pl.ds(col, HD)], target.at[n, h], sem.at[0]
                    )
                )
    for c in more:
        c.start()
    copies += more
    lane = lax.broadcasted_iota(jnp.int32, (BLK, HD), 1)
    row = lax.broadcasted_iota(jnp.int32, (BLK, HD), 0)
    lane_start = jnp.full((BLK, HD), nblk * BLK, jnp.int32)
    lane_end = lane_start
    for i in range(n_docs):
        lane_start = jnp.where(lane == i, starts[i], lane_start)
        lane_end = jnp.where(lane == i, ends[i], lane_end)
    lane_start, lane_end = lane_start - row, lane_end - row

    def inside(b):
        return (lane_start <= b * BLK) & (b * BLK < lane_end)

    def clear(b, carry):
        dk[b] = jnp.zeros(dk.shape[1:], dk.dtype)
        dv[b] = jnp.zeros(dv.shape[1:], dv.dtype)
        key_mask[b] = jnp.where(inside(b), 0.0, 1.0).astype(jnp.bfloat16)
        return carry

    lax.fori_loop(0, nblk, clear, 0)
    for c in copies:
        c.wait()

    def turn(b, carry):
        used = False
        for top, low in zip(query_blocks, firsts):
            used = used | ((b <= top) & (b >= low))

        @pl.when(used)
        def _():
            kt[b] = kv[b, :, :HD].T

        return carry

    lax.fori_loop(0, nblk, turn, 0)

    def choose(n, options):
        out = options[-1]
        for i in range(len(options) - 1):
            out = jnp.where(n == i, options[i], out)
        return out

    def span(i):
        n = i // heads
        b, lo = choose(n, query_blocks), choose(n, firsts)
        return b, lo, b - lo

    def prepare(i, b, bufs):
        qa, gt = bufs[:2]
        n, h = i // heads, lax.rem(i, heads)
        qa[:HD] = q[n, h].T
        qa[HD:] = jnp.where(inside(b), -FAR, 0.0).astype(jnp.bfloat16).T
        gt[...] = g[n, h].T

    def stats(tile, slot, bufs, state, causal, size):
        qa, gt, ebuf, dbuf, mbuf = bufs
        m, l, d = state
        rows = size * BLK
        kvs = kv[pl.ds(tile, size)].reshape(rows, 2 * HD)
        lhs = jnp.concatenate([kvs[:, :HD], key_mask[pl.ds(tile, size)].reshape(rows, HD)], axis=1)
        s = jnp.dot(lhs, qa[...], preferred_element_type=jnp.float32)
        if causal:
            key_at = lax.broadcasted_iota(jnp.int32, s.shape, 0)
            query_at = lax.broadcasted_iota(jnp.int32, s.shape, 1)
            s = jnp.where(key_at <= query_at, s, -FAR)
        dp = jnp.dot(kvs[:, HD:], gt[...], preferred_element_type=jnp.float32)
        step = BLK // 8 // CHUNKS
        s = s.reshape(size * CHUNKS, step, 8, BLK)
        dp = dp.reshape(size * CHUNKS, step, 8, BLK)
        for c in range(size * CHUNKS):
            at, part = slot + c // CHUNKS, pl.ds(c % CHUNKS * step, step)
            sc, dpc = s[c], dp[c]
            top = jnp.maximum(m, jnp.max(sc, axis=0))
            e = jnp.exp2((sc - top[None]) * EXP_SCALE)
            shrink = jnp.exp2((m - top) * EXP_SCALE)
            ebuf[at, part] = e
            dbuf[at, part] = dpc
            mbuf[at, c % CHUNKS] = top
            m, l, d = (
                top,
                l * shrink + jnp.sum(e, axis=0),
                d * shrink + jnp.sum(e * dpc, axis=0),
            )
        return (m, l, d)

    def grads(tile, slot, bufs, n, h, final, size):
        _, _, ebuf, dbuf, mbuf = bufs
        top, inverse, delta = final
        step = BLK // 8 // CHUNKS
        probs, scores = [], []
        for c in range(size * CHUNKS):
            at, part = slot + c // CHUNKS, pl.ds(c % CHUNKS * step, step)
            fix = jnp.exp2((mbuf[at, c % CHUNKS] - top) * EXP_SCALE) * inverse
            p = ebuf[at, part] * fix[None]
            ds = p * (dbuf[at, part] - delta[None])
            probs.append(p.reshape(BLK // CHUNKS, BLK).astype(jnp.bfloat16))
            scores.append(ds.reshape(BLK // CHUNKS, BLK).astype(jnp.bfloat16))
        p = jnp.concatenate(probs, axis=0)
        ds = jnp.concatenate(scores, axis=0)
        keys_t = jnp.concatenate([kt[tile + i] for i in range(size)], axis=1)
        dqt[...] += jnp.dot(keys_t, ds, preferred_element_type=jnp.float32)
        shape = (size, BLK, HD)
        dv[pl.ds(tile, size)] += jnp.dot(
            p, g[n, h], preferred_element_type=jnp.float32
        ).reshape(shape)
        dk[pl.ds(tile, size)] += jnp.dot(
            ds, q[n, h], preferred_element_type=jnp.float32
        ).reshape(shape)

    def finish(state):
        m, l, d = state
        top = jnp.max(m, axis=0, keepdims=True)
        shrink = jnp.exp2((m - top) * EXP_SCALE)
        inverse = 1.0 / jnp.sum(l * shrink, axis=0, keepdims=True)
        delta = jnp.sum(d * shrink, axis=0, keepdims=True) * inverse
        return (top, inverse, delta)

    none = jnp.full((8, BLK), -FAR, jnp.float32)
    zero = jnp.zeros((8, BLK), jnp.float32)
    fresh = (none, zero, zero)

    def sweep(low, high, body, state, size=2):
        full = (high - low) // size
        state = lax.fori_loop(0, full, lambda t, st: body(low + size * t, size, st), state)
        return lax.fori_loop(low + size * full, high, lambda t, st: body(t, 1, st), state)

    def start():
        b, lo, count = span(0)
        prepare(0, b, even)
        state = stats(b, count, even, fresh, True, 1)

        def only(t, size, state):
            return stats(lo + t, t, even, state, False, size)

        return finish(sweep(0, count, only, state))

    def step(i, final, now, later):
        n, h = i // heads, lax.rem(i, heads)
        nxt = jnp.minimum(i + 1, items - 1)
        b, lo, count = span(i)
        b_n, lo_n, count_n = span(nxt)
        todo = jnp.where(i + 1 < items, count_n, 0)
        both = jnp.minimum(count, todo)
        prepare(nxt, b_n, later)
        dqt[...] = jnp.zeros_like(dqt)
        state = stats(b_n, count_n, later, fresh, True, 1)
        grads(b, count, now, n, h, final, 1)

        def joint(t, size, state):
            state = stats(lo_n + t, t, later, state, False, size)
            grads(lo + t, t, now, n, h, final, size)
            return state

        def ahead(t, size, state):
            return stats(lo_n + t, t, later, state, False, size)

        def behind(t, size, carry):
            grads(lo + t, t, now, n, h, final, size)
            return carry

        state = sweep(0, both, joint, state, 3)
        state = sweep(both, todo, ahead, state)
        sweep(both, count, behind, 0)
        dq[n, h] = (dqt[...] * SCALE).T.astype(jnp.bfloat16)
        return finish(state)

    def pair(j, final):
        final = step(2 * j, final, even, odd)
        return step(2 * j + 1, final, odd, even)

    lax.fori_loop(0, items // 2, pair, start())

    back = []
    for n in range(blocks):
        at_row = pl.multiple_of(halves[n] * BLK, BLK)
        for h in range(heads):
            back.append(
                pltpu.make_async_copy(
                    dq.at[n, h],
                    (dq_own, dq_par)[n // half].at[pl.ds(at_row, BLK), pl.ds(h * HD, HD)],
                    osem.at[0],
                )
            )
    for c in back:
        c.start()
    for i in list(range(chips + N_Z, 2 * chips)) + list(range(N_Z, chips + N_Z)) + list(range(N_Z)):
        at = chip_at(1, i % chips, i >= chips)
        for first_row, block in ((0, at), (BLK, nblk - 1 - at)):
            stage[i, pl.ds(first_row, BLK), :HD] = (dk[block] * SCALE).astype(jnp.bfloat16)
            stage[i, pl.ds(first_row, BLK), HD:] = dv[block].astype(jnp.bfloat16)
        out = own_outs[i] if i < chips else par_outs[(i - chips) // N_Z].at[i % N_Z]
        c = pltpu.make_async_copy(stage.at[i], out, osem.at[0])
        c.start()
        back.append(c)
    for c in back:
        c.wait()


def run_attention(table, q_own, q_par, g_own, g_par, pieces):
    chips = len(pieces) // 2
    heads = q_own.shape[1] // HD // 2
    rows = q_own.shape[0]
    blocks, nblk = 2 * rows // BLK, 4 * chips
    hbm = pl.BlockSpec(memory_space=pl.ANY)
    smem = pl.BlockSpec(memory_space=pltpu.SMEM)
    bf16, f32 = jnp.bfloat16, jnp.float32
    part = jax.ShapeDtypeStruct((rows, 2 * HD), bf16)
    parts = jax.ShapeDtypeStruct((N_Z, rows, 2 * HD), bf16)
    grad = jax.ShapeDtypeStruct((rows, heads * HD), bf16)
    work = (
        pltpu.VMEM((2 * HD, BLK), bf16),
        pltpu.VMEM((HD, BLK), bf16),
        pltpu.VMEM((WINDOW, BLK // 8, 8, BLK), f32),
        pltpu.VMEM((WINDOW, BLK // 8, 8, BLK), f32),
        pltpu.VMEM((WINDOW, CHUNKS, 8, BLK), f32),
    )
    return pl.pallas_call(
        functools.partial(attention_kernel, blocks=blocks, heads=heads, chips=chips),
        out_shape=[part] * chips + [parts] * (chips // N_Z) + [grad] * 2,
        in_specs=[smem] + [hbm] * (4 + 2 * chips),
        out_specs=[hbm] * (chips + chips // N_Z + 2),
        scratch_shapes=[
            pltpu.VMEM((nblk, BLK, 2 * HD), bf16),
            pltpu.VMEM((nblk, BLK, HD), bf16),
            pltpu.VMEM((nblk, HD, BLK), bf16),
            pltpu.VMEM((nblk, BLK, HD), f32),
            pltpu.VMEM((nblk, BLK, HD), f32),
            pltpu.VMEM((blocks, heads, BLK, HD), bf16),
            pltpu.VMEM((blocks, heads, BLK, HD), bf16),
            pltpu.VMEM((blocks, heads, BLK, HD), bf16),
            pltpu.VMEM((HD, BLK), f32),
            pltpu.VMEM((2 * chips, rows, 2 * HD), bf16),
            work,
            work,
            pltpu.SemaphoreType.DMA((1,)),
            pltpu.SemaphoreType.DMA((1,)),
        ],
        compiler_params=pltpu.CompilerParams(vmem_limit_bytes=46 * 1024 * 1024,
       ),
        name="attention",
    )(table, q_own, q_par, g_own, g_par, *pieces)


def local(queries, keys, values, out_grad, doc_lengths, assignment):
    n_ctx = lax.axis_size("ctx")
    n_pipe = lax.axis_size("pipe")
    me = lax.axis_index("ctx")
    core = me % 2
    n_y = n_ctx // 2 // N_Z

    def hop(x, dy, dz):
        def to(i):
            y, z, c = i // (2 * N_Z), i // 2 % N_Z, i % 2
            return ((y + dy) % n_y) * 2 * N_Z + ((z + dz) % N_Z) * 2 + c

        return lax.ppermute(x, "ctx", [(i, to(i)) for i in range(n_ctx)])

    def swap(x):
        return lax.ppermute(x, "ctx", [(i, i ^ 1) for i in range(n_ctx)])

    q, g = queries[0], out_grad[0]
    packed = jnp.concatenate([keys[0], values[0]], axis=1)
    facing = hop(packed, 1, 0)
    near_in = [hop(packed, 0, dz) for dz in (1, 2, 3)]
    far_in = [hop(facing, 0, 1), hop(near_in[1], 1, 0), hop(facing, 0, 3)]
    mine = [packed] + near_in + [facing] + far_in
    q_par, g_par = swap(q), swap(g)
    others = [swap(x) for x in mine]

    results = run_attention(
        jnp.concatenate([me[None], assignment[0], doc_lengths[0]]).astype(jnp.int32),
        q,
        q_par,
        g,
        g_par,
        mine + others,
    )
    chips = len(mine)
    own_parts, par_parts = results[:chips], results[chips : chips + n_y]
    dq_own, dq_par = results[chips + n_y :]

    def route(flip):
        pairs = []
        for s in range(n_pipe):
            for i in range(n_ctx):
                to = (s - 1) % n_pipe * n_ctx + (i ^ 1 if flip else i)
                pairs.append((s * n_ctx + i, to))
        return pairs

    def total(parts):
        return functools.reduce(lambda a, b: a + b, [x.astype(jnp.float32) for x in parts])

    far_swap, near_swap = swap(par_parts[1]), swap(par_parts[0])
    dq_same = lax.ppermute(dq_own, ("pipe", "ctx"), route(False))
    dq_flip = lax.ppermute(dq_par, ("pipe", "ctx"), route(True))
    ahead = total([own_parts[N_Z + 2], far_swap[2]]).astype(jnp.bfloat16)
    ahead, far_swap = lax.optimization_barrier((ahead, far_swap))
    far = [total([own_parts[N_Z + i], far_swap[i]]).astype(jnp.bfloat16) for i in (0, 1, 3)]
    far = lax.optimization_barrier(far)
    far = [far[0], far[1], ahead, far[2]]
    far_in = [hop(far[dz], 0, dz) for dz in (1, 2, 3)]
    near = [total([own_parts[i], near_swap[i]]).astype(jnp.bfloat16) for i in range(N_Z)]
    near_in = [hop(near[dz], 0, dz) for dz in (1, 2, 3)]

    def across(x, dy):
        pairs = []
        for s in range(n_pipe):
            for i in range(n_ctx):
                to = (s - 1) % n_pipe * n_ctx + (i + dy * 2 * N_Z) % n_ctx
                pairs.append((s * n_ctx + i, to))
        return lax.ppermute(x, ("pipe", "ctx"), pairs)

    crossed = across(total([far[0]] + far_in).astype(jnp.bfloat16), 1)
    straight = across(total([near[0]] + near_in).astype(jnp.bfloat16), 0)
    k_out = total([crossed[:, :HD], straight[:, :HD]]).astype(jnp.bfloat16)
    v_out = total([crossed[:, HD:], straight[:, HD:]]).astype(jnp.bfloat16)
    left = jnp.where(core == 0, dq_same, dq_flip)
    right = jnp.where(core == 0, dq_flip, dq_same)
    q_out = jnp.concatenate([left, right], axis=1)
    return (q_out[None], k_out[None], v_out[None])


def solution(mesh):
    return step_of(mesh, local)


def step_of(mesh, body):
    return jax.shard_map(
        body,
        mesh=mesh,
        in_specs=(
            P("pipe", "ctx", None),
            P("pipe", "ctx", None),
            P("pipe", "ctx", None),
            P("pipe", "ctx", None),
            P("pipe", None),
            P("pipe", None),
        ),
        out_specs=(P("pipe", "ctx", None), P("pipe", "ctx", None), P("pipe", "ctx", None)),
        check_vma=False,
    )
```
